32 devices in a mesh: dp: 8 (over z, x), group: 4 (over y, core).
Axes of the slice: x: 2, y: 2, z: 4, core: 2. Of those that a mesh axis runs over, the one named last changes fastest.
Arguments:
- latents: bfloat16 [128, 256, 384], P(('dp', 'group')), may hold values from -40 to 40
- cotangent: bfloat16 [128, 256, 384], P(('dp', 'group')), may hold values from -6 to 6
- timestep: int32 [128], P(('dp', 'group')), may hold values from 0 to 999
- labels: int32 [128], P(('dp', 'group')), may hold values from 0 to 1000
- class_table: bfloat16 [1001, 384], replicated, may hold values from -6 to 6
- input_proj: float32 [384, 4992], P('dp'), may hold values from -4 to 4
- attn_proj: float32 [384, 384], P('dp'), may hold values from -0.3125 to 0.3125
- mlp_down: float32 [1536, 384], P('dp'), may hold values from -0.15625 to 0.15625
- biases: float32 [5376], P('dp'), may hold values from -0.18 to 0.18
- mean_input: float32 [384, 4992], P('dp'), may hold values from -108.6116 to 108.6116
- mean_attn: float32 [384, 384], P('dp'), may hold values from -108.6116 to 108.6116
- mean_down: float32 [1536, 384], P('dp'), may hold values from -108.6116 to 108.6116
- mean_biases: float32 [5376], P('dp'), may hold values from -108.6116 to 108.6116
- sq_input: float32 [384, 4992], P('dp'), may hold values from 0.98304 to 98.304
- sq_attn: float32 [384, 384], P('dp'), may hold values from 0.98304 to 98.304
- sq_down: float32 [1536, 384], P('dp'), may hold values from 0.98304 to 98.304
- sq_biases: float32 [5376], P('dp'), may hold values from 0.98304 to 98.304
Outputs:
- block_out: bfloat16 [128, 256, 384], P(('dp', 'group'))
- grad_latents: float32 [128, 256, 384], P(('dp', 'group'))
- grad_cond: float32 [128, 384], P(('dp', 'group'))
- grad_input: float32 [384, 4992], P('dp')
- grad_attn: float32 [384, 384], P('dp')
- grad_down: float32 [1536, 384], P('dp')
- grad_biases: float32 [5376], P('dp')
- new_input: float32 [384, 4992], P('dp')
- new_attn: float32 [384, 384], P('dp')
- new_down: float32 [1536, 384], P('dp')
- new_biases: float32 [5376], P('dp')
- new_mean_input: float32 [384, 4992], P('dp')
- new_mean_attn: float32 [384, 384], P('dp')
- new_mean_down: float32 [1536, 384], P('dp')
- new_mean_biases: float32 [5376], P('dp')
- new_sq_input: float32 [384, 4992], P('dp')
- new_sq_attn: float32 [384, 384], P('dp')
- new_sq_down: float32 [1536, 384], P('dp')
- new_sq_biases: float32 [5376], P('dp')
The draws below stay inside these ranges and needn't reach their ends.
All inputs are finite; a program needn't handle non-finite values.
Results may differ from the reference program's by a relative error of at most 0.012.
The reference program's roundings to bfloat16 on the way count: a program that leaves them out, or rounds other values in their place, can miss the bound.
Values may be sent and summed in bfloat16 or wider, within the bound.
No kernel may reach another device: no remote copies, remote signals or barrier semaphores. Data moves between devices by JAX's collectives and lax.ppermute only.
A program may use at most 128 MiB of HBM per device.

```python
import math
import jax
import jax.numpy as jnp
from jax import lax

D = 384
HEAD = 64
FF = 1536
NCLASS = 1001
SEQ = 256
STEP = 2
BATCH = 128
IN_COLS = 4992
NBIAS = 5376
TOKENS_ALL = 32768


def draw_latents(key, part):
    keys = jax.random.split(key, 3)
    shape = (BATCH, SEQ, D)
    base = jax.random.normal(keys[0], shape, jnp.float32)
    row_scale = jnp.exp(jax.random.uniform(keys[1], (BATCH, SEQ, 1), jnp.float32, -0.7, 0.7))
    col_scale = jnp.exp(jax.random.uniform(keys[2], (1, 1, D), jnp.float32, -0.7, 0.7))
    return jnp.clip(base * row_scale * col_scale, -40.0, 40.0).astype(jnp.bfloat16)


def draw_input_proj(key, part):
    columns = 9 * D + FF
    base = jax.random.normal(key, (D, columns), jnp.float32) / math.sqrt(D)
    return jnp.clip(base, -4.0, 4.0)


def plant(values, own_key, low, largest):
    longest = values.shape.index(max(values.shape))
    spots = []
    for shift in (0, 1):
        where = [jax.random.randint(jax.random.fold_in(own_key, axis), (), 0, length) for axis, length in enumerate(values.shape)]
        where[longest] = (where[longest] + shift) % values.shape[longest]
        spots.append(tuple(where))
    return values.at[spots[0]].set(low).at[spots[1]].set(largest)


def levels(rng, extent, shards, smallest, largest):
    level, own = 1.0, jax.random.fold_in(rng, 6)
    for axis_at, shards_of in shards:
        draws = jnp.exp(jax.random.uniform(jax.random.fold_in(own, axis_at), (shards_of,), jnp.float32, smallest / len(shards), largest / len(shards)))
        level = level * jnp.repeat(draws, extent[axis_at] // shards_of).reshape([-1 if axis == axis_at else 1 for axis in range(len(extent))])
    return level


def bell_draw(rng, dims, spread, most, cuts=(), kind=jnp.bfloat16):
    gain = levels(rng, dims, cuts, -0.22, 0.18) if cuts else 1.0
    values = jax.random.normal(rng, dims, jnp.float32) * spread * gain
    return jnp.minimum(jnp.maximum(values, -most), most).astype(kind)


def setup_inputs(seed: int = 0) -> dict:
    splits = jax.random.split(jax.random.key(seed), 18)
    return {
        "latents": draw_latents(jax.random.fold_in(splits[17], 71), 0),
        "cotangent": bell_draw(splits[1], (BATCH, SEQ, D), 1.0, 6.0, ((0, 32),)),
        "timestep": plant(jax.random.randint(splits[2], (BATCH,), 0, 1000), jax.random.fold_in(splits[2], 1), 0, 999).astype(jnp.int32),
        "labels": plant(jax.random.randint(splits[3], (BATCH,), 0, NCLASS), jax.random.fold_in(splits[3], 1), 0, NCLASS - 1).astype(jnp.int32),
        "class_table": bell_draw(splits[4], (NCLASS, D), 1.0, 6.0),
        "input_proj": draw_input_proj(jax.random.fold_in(splits[17], 71), 0),
        "attn_proj": bell_draw(splits[6], (D, D), D ** -0.5, 0.3125, ((0, 8),), jnp.float32),
        "mlp_down": bell_draw(splits[7], (FF, D), FF ** -0.5, 0.15625, ((0, 8),), jnp.float32),
        "biases": bell_draw(splits[8], (NBIAS,), 0.03, 0.18, ((0, 8),), jnp.float32),
        "mean_input": bell_draw(splits[9], (D, IN_COLS), (0.1 * TOKENS_ALL ** 0.5), 108.6116, ((0, 8),), jnp.float32),
        "mean_attn": bell_draw(splits[10], (D, D), (0.1 * TOKENS_ALL ** 0.5), 108.6116, ((0, 8),), jnp.float32),
        "mean_down": bell_draw(splits[11], (FF, D), (0.1 * TOKENS_ALL ** 0.5), 108.6116, ((0, 8),), jnp.float32),
        "mean_biases": bell_draw(splits[12], (NBIAS,), (0.1 * TOKENS_ALL ** 0.5), 108.6116, ((0, 8),), jnp.float32),
        "sq_input": jnp.clip(jnp.exp(math.log(98.304) - 4.6051702 * jax.random.uniform(splits[13], (D, IN_COLS), jnp.float32) ** levels(splits[13], (D, IN_COLS), ((0, 8),), -0.2, 0.2)), 0.98304, 98.304),
        "sq_attn": jnp.clip(jnp.exp(math.log(98.304) - 4.6051702 * jax.random.uniform(splits[14], (D, D), jnp.float32) ** levels(splits[14], (D, D), ((0, 8),), -0.2, 0.2)), 0.98304, 98.304),
        "sq_down": jnp.clip(jnp.exp(math.log(98.304) - 4.6051702 * jax.random.uniform(splits[15], (FF, D), jnp.float32) ** levels(splits[15], (FF, D), ((0, 8),), -0.2, 0.2)), 0.98304, 98.304),
        "sq_biases": jnp.clip(jnp.exp(math.log(98.304) - 4.6051702 * jax.random.uniform(splits[16], (NBIAS,), jnp.float32) ** levels(splits[16], (NBIAS,), ((0, 8),), -0.2, 0.2)), 0.98304, 98.304),
    }


learn_rate = 0.01
beta_one = 0.9
beta_two = 0.999
adam_eps = 1e-08
norm_eps = 1e-06

def time_embed(timestep, model_width):
    half_width = model_width // 2
    frequency = jnp.exp(jnp.arange(half_width, dtype=jnp.float32) * (-math.log(10000.0) / half_width))
    angles = timestep.astype(jnp.float32)[:, None] * frequency[None, :]
    return jnp.concatenate([jnp.cos(angles), jnp.sin(angles)], axis=1)

def layer_norm(values):
    row_mean = lax.optimization_barrier(jnp.mean(values, axis=-1, keepdims=True))
    centred = values - row_mean
    inv_std = lax.rsqrt(lax.optimization_barrier(jnp.mean(centred * centred, axis=-1, keepdims=True)) + norm_eps)
    return (centred * inv_std, inv_std)

def norm_back(gradient, normed, inv_std):
    return inv_std * (gradient - lax.optimization_barrier(jnp.mean(gradient, axis=-1, keepdims=True)) - normed * lax.optimization_barrier(jnp.mean(gradient * normed, axis=-1, keepdims=True)))

def gelu_parts(preact):
    inner_scale = math.sqrt(2.0 / math.pi)
    tangent = jnp.tanh(inner_scale * (preact + 0.044715 * preact * preact * preact))
    result = 0.5 * preact * (1.0 + tangent)
    slope = 0.5 * (1.0 + tangent) + 0.5 * preact * (1.0 - tangent * tangent) * inner_scale * (1.0 + 3.0 * 0.044715 * preact * preact)
    return (result, slope)

def adam_step(weight, moment, second, gradient):
    moment = beta_one * moment + (1.0 - beta_one) * gradient
    second = beta_two * second + (1.0 - beta_two) * gradient * gradient
    first_fix = 1.0 - beta_one ** STEP
    second_fix = 1.0 - beta_two ** STEP
    weight = weight - learn_rate * (moment / first_fix) / (jnp.sqrt(second / second_fix) + adam_eps)
    return (weight, moment, second)

def latent_block(latents, cotangent, timestep, labels, class_table, input_proj, attn_proj, mlp_down, biases):
    latent_count, seq_len, model_width = latents.shape
    hidden_width = mlp_down.shape[0]
    head_count = model_width // HEAD
    row_count = latent_count * seq_len
    scale = 1.0 / math.sqrt(HEAD)
    head_shape = (latent_count, seq_len, head_count, HEAD)
    bias_all = biases.astype(jnp.float32)
    bias_query = bias_all[:model_width]
    bias_value = bias_all[model_width:2 * model_width]
    bias_attn = bias_all[2 * model_width:3 * model_width]
    bias_up = bias_all[3 * model_width:3 * model_width + hidden_width]
    bias_down = bias_all[3 * model_width + hidden_width:4 * model_width + hidden_width]
    bias_mod = bias_all[4 * model_width + hidden_width:]
    w_qkv = input_proj[:, :3 * model_width]
    w_up = input_proj[:, 3 * model_width:3 * model_width + hidden_width]
    w_mod = input_proj[:, 3 * model_width + hidden_width:]
    condition = time_embed(timestep, model_width) + class_table[labels].astype(jnp.float32)
    sigmoid_c = jax.nn.sigmoid(condition)
    cond_act = (condition * sigmoid_c).astype(jnp.bfloat16)
    modulation = jnp.dot(cond_act, w_mod, preferred_element_type=jnp.float32) + bias_mod
    shift_a, scale_a, gate_a, shift_m, scale_m, gate_m = [modulation[:, None, part_index * model_width:(part_index + 1) * model_width] for part_index in range(6)]
    residual_in = latents.astype(jnp.float32)
    normed_a, inv_std_a = layer_norm(residual_in)
    input_a = (normed_a * (1.0 + scale_a) + shift_a).astype(jnp.bfloat16).reshape(row_count, model_width)
    projected = jnp.dot(input_a, w_qkv, preferred_element_type=jnp.float32)
    queries = (projected[:, :model_width] + bias_query).astype(jnp.bfloat16).reshape(head_shape)
    key_vecs = projected[:, model_width:2 * model_width].astype(jnp.bfloat16).reshape(head_shape)
    values = (projected[:, 2 * model_width:] + bias_value).astype(jnp.bfloat16).reshape(head_shape)
    scores = jnp.einsum('lqhe,lkhe->lhqk', queries.astype(jnp.float32), key_vecs.astype(jnp.float32)) * scale
    row_peak = lax.optimization_barrier(jnp.max(scores, axis=-1, keepdims=True))
    log_total = row_peak + jnp.log(lax.optimization_barrier(jnp.sum(jnp.exp(scores - row_peak), axis=-1, keepdims=True)))
    attn_probs = jnp.exp(scores - log_total)
    probs_b = attn_probs.astype(jnp.bfloat16)
    attended = jnp.einsum('lhqk,lkhe->lqhe', probs_b.astype(jnp.float32), values.astype(jnp.float32)).astype(jnp.bfloat16).reshape(row_count, model_width)
    branch_a = (jnp.dot(attended, attn_proj, preferred_element_type=jnp.float32) + bias_attn).reshape(latent_count, seq_len, model_width)
    middle = residual_in + gate_a * branch_a
    normed_m, inv_std_m = layer_norm(middle)
    input_m = (normed_m * (1.0 + scale_m) + shift_m).astype(jnp.bfloat16).reshape(row_count, model_width)
    preact = jnp.dot(input_m, w_up, preferred_element_type=jnp.float32) + bias_up
    gelu_out, slope = gelu_parts(preact)
    gelu_b = gelu_out.astype(jnp.bfloat16)
    branch_m = (jnp.dot(gelu_b, mlp_down, preferred_element_type=jnp.float32) + bias_down).reshape(latent_count, seq_len, model_width)
    block_out = (middle + gate_m * branch_m).astype(jnp.bfloat16)
    grad_out = cotangent.astype(jnp.float32)
    d_gate_m = lax.optimization_barrier(jnp.sum(grad_out * branch_m, axis=1))
    d_branch_m = (grad_out * gate_m).reshape(row_count, model_width)
    d_branch_mb = d_branch_m.astype(jnp.bfloat16)
    grad_down = jnp.dot(gelu_b.T, d_branch_mb, preferred_element_type=jnp.float32)
    grad_bias_down = lax.optimization_barrier(jnp.sum(d_branch_m, axis=0))
    d_preact = jnp.dot(d_branch_mb, mlp_down.T, preferred_element_type=jnp.float32) * slope
    d_preact_b = d_preact.astype(jnp.bfloat16)
    grad_up = jnp.dot(input_m.T, d_preact_b, preferred_element_type=jnp.float32)
    grad_bias_up = lax.optimization_barrier(jnp.sum(d_preact, axis=0))
    d_input_m = jnp.dot(d_preact_b, w_up.T, preferred_element_type=jnp.float32).reshape(latent_count, seq_len, model_width)
    d_scale_m = lax.optimization_barrier(jnp.sum(d_input_m * normed_m, axis=1))
    d_shift_m = lax.optimization_barrier(jnp.sum(d_input_m, axis=1))
    d_middle = grad_out + norm_back(d_input_m * (1.0 + scale_m), normed_m, inv_std_m)
    d_gate_a = lax.optimization_barrier(jnp.sum(d_middle * branch_a, axis=1))
    d_branch_a = (d_middle * gate_a).reshape(row_count, model_width)
    d_branch_ab = d_branch_a.astype(jnp.bfloat16)
    grad_attn = jnp.dot(attended.T, d_branch_ab, preferred_element_type=jnp.float32)
    grad_bias_attn = lax.optimization_barrier(jnp.sum(d_branch_a, axis=0))
    d_attended = jnp.dot(d_branch_ab, attn_proj.T, preferred_element_type=jnp.float32).astype(jnp.bfloat16).reshape(head_shape)
    d_values = jnp.einsum('lhqk,lqhe->lkhe', probs_b.astype(jnp.float32), d_attended.astype(jnp.float32))
    d_probs = jnp.einsum('lqhe,lkhe->lhqk', d_attended.astype(jnp.float32), values.astype(jnp.float32))
    delta = lax.optimization_barrier(jnp.sum(attn_probs * d_probs, axis=-1, keepdims=True))
    d_scores = (attn_probs * (d_probs - delta) * scale).astype(jnp.bfloat16)
    d_queries = jnp.einsum('lhqk,lkhe->lqhe', d_scores.astype(jnp.float32), key_vecs.astype(jnp.float32))
    d_keys = jnp.einsum('lhqk,lqhe->lkhe', d_scores.astype(jnp.float32), queries.astype(jnp.float32))
    d_projected = jnp.concatenate([d_queries.reshape(row_count, model_width), d_keys.reshape(row_count, model_width), d_values.reshape(row_count, model_width)], axis=1)
    d_projected_b = d_projected.astype(jnp.bfloat16)
    grad_qkv = jnp.dot(input_a.T, d_projected_b, preferred_element_type=jnp.float32)
    grad_bias_query = lax.optimization_barrier(jnp.sum(d_projected[:, :model_width], axis=0))
    grad_bias_value = lax.optimization_barrier(jnp.sum(d_projected[:, 2 * model_width:], axis=0))
    d_input_a = jnp.dot(d_projected_b, w_qkv.T, preferred_element_type=jnp.float32).reshape(latent_count, seq_len, model_width)
    d_scale_a = lax.optimization_barrier(jnp.sum(d_input_a * normed_a, axis=1))
    d_shift_a = lax.optimization_barrier(jnp.sum(d_input_a, axis=1))
    grad_latents = d_middle + norm_back(d_input_a * (1.0 + scale_a), normed_a, inv_std_a)
    d_modulation = jnp.concatenate([d_shift_a, d_scale_a, d_gate_a, d_shift_m, d_scale_m, d_gate_m], axis=1)
    d_modulation_b = d_modulation.astype(jnp.bfloat16)
    grad_mod = jnp.dot(cond_act.T, d_modulation_b, preferred_element_type=jnp.float32)
    grad_bias_mod = lax.optimization_barrier(jnp.sum(d_modulation, axis=0))
    grad_cond = jnp.dot(d_modulation_b, w_mod.T, preferred_element_type=jnp.float32) * (sigmoid_c * (1.0 + condition * (1.0 - sigmoid_c)))
    grad_input = jnp.concatenate([grad_qkv, grad_up, grad_mod], axis=1)
    grad_biases = jnp.concatenate([grad_bias_query, grad_bias_value, grad_bias_attn, grad_bias_up, grad_bias_down, grad_bias_mod])
    return (block_out, grad_latents, grad_cond, (grad_input, grad_attn, grad_down, grad_biases))

def reference(latents, cotangent, timestep, labels, class_table, input_proj, attn_proj, mlp_down, biases, mean_input, mean_attn, mean_down, mean_biases, sq_input, sq_attn, sq_down, sq_biases):
    working = (input_proj.astype(jnp.bfloat16), attn_proj.astype(jnp.bfloat16), mlp_down.astype(jnp.bfloat16), biases.astype(jnp.bfloat16))
    block_size = math.gcd(BATCH, max(1, 4096 // SEQ))
    block_count = BATCH // block_size

    def per_block(totals, block_index):
        row_start = (block_index * block_size).astype(jnp.int32)
        pick = lambda array: lax.dynamic_slice_in_dim(array, row_start, block_size, 0)
        block_out, grad_latents, grad_cond, gradients = latent_block(pick(latents), pick(cotangent), pick(timestep), pick(labels), class_table, working[0], working[1], working[2], working[3])
        totals = tuple((total + gradient for total, gradient in zip(totals, gradients)))
        return (totals, (block_out, grad_latents, grad_cond))
    zero_grads = tuple((jnp.zeros(array.shape, jnp.float32) for array in (input_proj, attn_proj, mlp_down, biases)))
    totals, stacked = lax.scan(per_block, zero_grads, jnp.arange(block_count, dtype=jnp.int32))
    block_out = stacked[0].reshape(BATCH, SEQ, D)
    grad_latents = stacked[1].reshape(BATCH, SEQ, D)
    grad_cond = stacked[2].reshape(BATCH, D)
    new_input, new_mean_input, new_sq_input = adam_step(input_proj, mean_input, sq_input, totals[0])
    new_attn, new_mean_attn, new_sq_attn = adam_step(attn_proj, mean_attn, sq_attn, totals[1])
    new_down, new_mean_down, new_sq_down = adam_step(mlp_down, mean_down, sq_down, totals[2])
    new_biases, new_mean_biases, new_sq_biases = adam_step(biases, mean_biases, sq_biases, totals[3])
    return (block_out, grad_latents, grad_cond, totals[0], totals[1], totals[2], totals[3], new_input, new_attn, new_down, new_biases, new_mean_input, new_mean_attn, new_mean_down, new_mean_biases, new_sq_input, new_sq_attn, new_sq_down, new_sq_biases)
```

```python
import functools
import math

import jax
import jax.numpy as jnp
from jax import lax
from jax.experimental import pallas as pl
from jax.experimental.pallas import tpu as pltpu
from jax.sharding import PartitionSpec as P

HEAD = 64
STEP = 2
GROUP = 4

learn_rate = 0.01
beta_one = 0.9
beta_two = 0.999
adam_eps = 1e-08
norm_eps = 1e-06

f32 = jnp.float32
bf16 = jnp.bfloat16

NN = (((1,), (0,)), ((), ()))
NT = (((1,), (1,)), ((), ()))
TN = (((0,), (0,)), ((), ()))


def dot(left, right, dims=NN):
    return lax.dot_general(left, right, dims, preferred_element_type=f32)


def row_mean(values):
    return jnp.sum(values, axis=-1, keepdims=True) * (1.0 / values.shape[-1])


def layer_norm(values):
    centred = values - row_mean(values)
    inv_std = lax.rsqrt(row_mean(centred * centred) + norm_eps)
    return centred * inv_std, inv_std


def norm_back(gradient, normed, inv_std):
    return inv_std * (gradient - row_mean(gradient) - normed * row_mean(gradient * normed))


def token_sum(values):
    return jnp.sum(values, axis=0, keepdims=True)


def time_embed(timestep, model_width):
    half_width = model_width // 2
    frequency = jnp.exp(
        jnp.arange(half_width, dtype=f32) * (-math.log(10000.0) / half_width)
    )
    angles = timestep.astype(f32)[:, None] * frequency[None, :]
    return jnp.concatenate([jnp.cos(angles), jnp.sin(angles)], axis=1)


def unpack_columns(place, pieces, whole):
    owners, rows, width = pieces[0].shape
    me, mine = place[0], place[1]
    for block in range(GROUP):
        for k in range(GROUP):

            @pl.when((mine ^ k) == block)
            def _():
                for owner in range(owners):
                    whole[owner * rows : (owner + 1) * rows, block * width : (block + 1) * width] = (
                        pieces[k][owner ^ me]
                    )


def unpack_rows(place, pieces, whole):
    owners, rows, width = pieces[0].shape
    me, mine = place[0], place[1]
    for block in range(GROUP):
        for k in range(GROUP):

            @pl.when((mine ^ k) == block)
            def _():
                for owner in range(owners):
                    start = (owner * GROUP + block) * rows
                    whole[start : start + rows, :] = pieces[k][owner ^ me]


def pack_block(place, block, owner, value, keep, send):
    k = place[1] ^ block
    spot = place[0] ^ owner
    half = k >> 1

    @pl.when((k & 1) == 0)
    def _():
        keep[half, spot] = value

    @pl.when((k & 1) == 1)
    def _():
        send[half, spot] = value.astype(bf16)


def lane_masks():
    lane = lax.broadcasted_iota(jnp.int32, (1, 2 * HEAD), 1)
    low = (lane < HEAD).astype(f32)
    return low.astype(bf16), (1.0 - low).astype(bf16)


def attn_forward(place, lat, mod, bias, p0, p1, p2, p3, qkv_o, att_o, branch_o, lse_o, whole, att_t):
    width = lat.shape[-1]

    @pl.when(pl.program_id(0) == 0)
    def _():
        unpack_columns(place, (p0, p1, p2, p3), whole)

    normed, _ = layer_norm(lat[0].astype(f32))
    input_a = (normed * (1.0 + mod[0, 1:2]) + mod[0, 0:1]).astype(bf16)
    projected = dot(input_a, whole[:, : 3 * width])
    queries = (projected[:, :width] + bias[0:1, :width]).astype(bf16)
    key_vecs = projected[:, width : 2 * width].astype(bf16)
    values = (projected[:, 2 * width :] + bias[0:1, width : 2 * width]).astype(bf16)
    qkv_o[0, :, :width] = queries
    qkv_o[0, :, width : 2 * width] = key_vecs
    qkv_o[0, :, 2 * width :] = values
    values_t = values.T
    scale = 1.0 / math.sqrt(HEAD)
    masks = lane_masks()
    for pair in range(width // (2 * HEAD)):
        cols = slice(pair * 2 * HEAD, (pair + 1) * 2 * HEAD)
        for side in range(2):
            head = pair * 2 + side
            scores = dot(key_vecs[:, cols] * masks[side], queries[:, cols], NT) * scale
            peak = jnp.max(scores, axis=0, keepdims=True)
            powers = jnp.exp(scores - peak)
            total = jnp.sum(powers, axis=0, keepdims=True)
            lse_o[0, head : head + 1, :] = peak + jnp.log(total)
            probs = (powers * (1.0 / total)).astype(bf16)
            att_t[head * HEAD : (head + 1) * HEAD, :] = dot(
                values_t[head * HEAD : (head + 1) * HEAD, :], probs
            )
    attended = att_t[...].T.astype(bf16)
    att_o[0] = attended
    branch_o[0] = dot(attended, whole[:, 3 * width :]) + bias[0:1, 2 * width : 3 * width]


def mlp_both(
    place, lat, cot, branch, att, mod, bias,
    u0, u1, u2, u3, w0, w1, w2, w3,
    out_o, dmid_o, dmod_o, gattn_o, gbias_o, upk_o, ups_o, dnk_o, dns_o,
    w_up, w_down, gelu_s, slope_s, dpre_s, acc_up, acc_down,
):
    width = lat.shape[-1]
    hidden = w_up.shape[1]
    step = pl.program_id(0)
    first = step == 0

    @pl.when(first)
    def _():
        unpack_columns(place, (u0, u1, u2, u3), w_up)
        unpack_rows(place, (w0, w1, w2, w3), w_down)
        acc_up[...] = jnp.zeros_like(acc_up)
        acc_down[...] = jnp.zeros_like(acc_down)
        gattn_o[...] = jnp.zeros_like(gattn_o)
        gbias_o[...] = jnp.zeros_like(gbias_o)

    b_up = bias[0:1, 3 * width : 3 * width + hidden]
    b_down = bias[0:1, 3 * width + hidden : 4 * width + hidden]
    gate_a, shift_m, scale_m, gate_m = mod[0, 2:3], mod[0, 3:4], mod[0, 4:5], mod[0, 5:6]
    branch_a = branch[0]
    middle = lat[0].astype(f32) + gate_a * branch_a
    normed, inv_std = layer_norm(middle)
    input_m = (normed * (1.0 + scale_m) + shift_m).astype(bf16)
    inner = math.sqrt(2.0 / math.pi)
    chunk = 512
    for start in range(0, hidden, chunk):
        cols = slice(start, start + chunk)
        pre = dot(input_m, w_up[:, cols]) + b_up[:, cols]
        square = pre * pre
        tangent = jnp.tanh(pre * (inner + (inner * 0.044715) * square))
        upper = 0.5 * (1.0 + tangent)
        gelu_s[:, cols] = (pre * upper).astype(bf16)
        slope_s[:, cols] = upper + (0.5 * pre) * (1.0 - tangent * tangent) * (
            inner + (inner * 3.0 * 0.044715) * square
        )
    branch_m = dot(gelu_s[...], w_down[...]) + b_down
    out_o[0] = (middle + gate_m * branch_m).astype(bf16)
    grad_out = cot[0].astype(f32)
    dmod_o[0, 5:6] = token_sum(grad_out * branch_m)
    d_branch_m = grad_out * gate_m
    d_branch_mb = d_branch_m.astype(bf16)
    acc_down[...] += dot(d_branch_mb, gelu_s[...], TN)
    gbias_o[0:1, 3 * width + hidden : 4 * width + hidden] += token_sum(d_branch_m)
    for start in range(0, hidden, chunk):
        cols = slice(start, start + chunk)
        d_pre = dot(d_branch_mb, w_down[cols, :], NT) * slope_s[:, cols]
        gbias_o[0:1, 3 * width + start : 3 * width + start + chunk] += token_sum(d_pre)
        dpre_s[:, cols] = d_pre.astype(bf16)
    acc_up[...] += dot(input_m, dpre_s[...], TN)
    d_input = dot(dpre_s[...], w_up[...], NT)
    dmod_o[0, 4:5] = token_sum(d_input * normed)
    dmod_o[0, 3:4] = token_sum(d_input)
    d_middle = grad_out + norm_back(d_input * (1.0 + scale_m), normed, inv_std)
    dmid_o[0] = d_middle
    dmod_o[0, 2:3] = token_sum(d_middle * branch_a)
    d_branch_a = d_middle * gate_a
    gbias_o[0:1, 2 * width : 3 * width] += token_sum(d_branch_a)
    gattn_o[...] += dot(att[0], d_branch_a.astype(bf16), TN)

    @pl.when(step == pl.num_programs(0) - 1)
    def _():
        owners, rows = upk_o.shape[1], upk_o.shape[2]
        for block in range(GROUP):
            for owner in range(owners):
                value = acc_up[owner * rows : (owner + 1) * rows, block * width : (block + 1) * width]
                pack_block(place, block, owner, value, upk_o, ups_o)
        whole_down = acc_down[...].T
        for block in range(GROUP):
            for owner in range(owners):
                start = (owner * GROUP + block) * rows
                pack_block(place, block, owner, whole_down[start : start + rows, :], dnk_o, dns_o)


def attn_backward(
    place, lat, dmid, qkv, lse, mod, gattn, p0, p1, p2, p3,
    glat_o, dmod_o, gbias_o, keep_o, send_o,
    whole, dq_t, dproj, acc,
):
    width = lat.shape[-1]
    step = pl.program_id(0)

    @pl.when(step == 0)
    def _():
        unpack_columns(place, (p0, p1, p2, p3), whole)
        acc[...] = jnp.zeros_like(acc)
        gbias_o[...] = jnp.zeros_like(gbias_o)

    shift_a, scale_a, gate_a = mod[0, 0:1], mod[0, 1:2], mod[0, 2:3]
    normed, inv_std = layer_norm(lat[0].astype(f32))
    input_a = (normed * (1.0 + scale_a) + shift_a).astype(bf16)
    d_middle = dmid[0]
    d_att = dot((d_middle * gate_a).astype(bf16), whole[:, 3 * width :], NT).astype(bf16)
    scale = 1.0 / math.sqrt(HEAD)
    masks = lane_masks()
    low = lax.broadcasted_iota(jnp.int32, (1, 2 * HEAD), 1) < HEAD
    keys_t = qkv[0, :, width : 2 * width].T
    for pair in range(width // (2 * HEAD)):
        cols = slice(pair * 2 * HEAD, (pair + 1) * 2 * HEAD)
        q_pair = qkv[0, :, pair * 2 * HEAD : (pair + 1) * 2 * HEAD]
        k_pair = qkv[0, :, width + pair * 2 * HEAD : width + (pair + 1) * 2 * HEAD]
        v_pair = qkv[0, :, 2 * width + pair * 2 * HEAD : 2 * width + (pair + 1) * 2 * HEAD]
        do_pair = d_att[:, cols]
        d_keys, d_values = [], []
        for side in range(2):
            head = pair * 2 + side
            scores = dot(k_pair * masks[side], q_pair, NT) * scale
            probs = jnp.exp(scores - lse[0, head : head + 1, :])
            d_values.append(dot(probs.astype(bf16), do_pair))
            d_probs = dot(v_pair * masks[side], do_pair, NT)
            delta = jnp.sum(probs * d_probs, axis=0, keepdims=True)
            d_scores = (probs * (d_probs - delta) * scale).astype(bf16)
            d_keys.append(dot(d_scores, q_pair))
            dq_t[head * HEAD : (head + 1) * HEAD, :] = dot(
                keys_t[head * HEAD : (head + 1) * HEAD, :], d_scores
            )
        d_key = jnp.where(low, d_keys[0], d_keys[1])
        d_value = jnp.where(low, d_values[0], d_values[1])
        dproj[:, width + pair * 2 * HEAD : width + (pair + 1) * 2 * HEAD] = d_key.astype(bf16)
        dproj[:, 2 * width + pair * 2 * HEAD : 2 * width + (pair + 1) * 2 * HEAD] = d_value.astype(
            bf16
        )
        gbias_o[0:1, width + pair * 2 * HEAD : width + (pair + 1) * 2 * HEAD] += token_sum(d_value)
    d_query = dq_t[...].T
    gbias_o[0:1, :width] += token_sum(d_query)
    dproj[:, :width] = d_query.astype(bf16)
    acc[...] += dot(input_a, dproj[...], TN)
    d_input = dot(dproj[...], whole[:, : 3 * width], NT)
    dmod_o[0, 1:2] = token_sum(d_input * normed)
    dmod_o[0, 0:1] = token_sum(d_input)
    glat_o[0] = d_middle + norm_back(d_input * (1.0 + scale_a), normed, inv_std)

    @pl.when(step == pl.num_programs(0) - 1)
    def _():
        owners, rows = keep_o.shape[1], keep_o.shape[2]
        for block in range(GROUP):
            for owner in range(owners):
                span = slice(owner * rows, (owner + 1) * rows)
                if block < GROUP - 1:
                    value = acc[span, block * width : (block + 1) * width]
                else:
                    value = gattn[span, :]
                pack_block(place, block, owner, value, keep_o, send_o)


def adam_parts(weight, moment, second, gradient):
    moment = beta_one * moment + (1.0 - beta_one) * gradient
    second = beta_two * second + (1.0 - beta_two) * gradient * gradient
    first_fix = 1.0 - beta_one**STEP
    second_fix = 1.0 - beta_two**STEP
    weight = weight - (learn_rate / first_fix) * moment / (
        jnp.sqrt(second * (1.0 / second_fix)) + adam_eps
    )
    return weight, moment, second


def adam_kernel(place, *refs):
    (att0, att1, up0, up1, dn0, dn1, gmod, gbias) = refs[:8]
    weights, means, squares = refs[8:12], refs[12:16], refs[16:20]
    grads, new_w, new_m, new_s = refs[20:24], refs[24:28], refs[28:32], refs[32:36]
    width = att0.shape[-1]

    def write(which, where, gradient):
        grads[which][where] = gradient
        result = adam_parts(
            weights[which][where], means[which][where], squares[which][where], gradient
        )
        new_w[which][where], new_m[which][where], new_s[which][where] = result

    def block_of(same, other, block):
        k = place[1] ^ block
        mine = jnp.where((k & 2) == 0, same[0], same[1])
        theirs = jnp.where((k & 2) == 0, other[0], other[1])
        return jnp.where((k & 1) == 0, mine, theirs)

    everything = slice(None)
    for block in range(GROUP):
        g_att = block_of(att0, att1, block)
        if block < GROUP - 1:
            write(0, (everything, slice(block * width, (block + 1) * width)), g_att)
        else:
            write(1, (everything, everything), g_att)
        at = (GROUP - 1 + block) * width
        write(0, (everything, slice(at, at + width)), block_of(up0, up1, block))
        write(2, (block,), block_of(dn0, dn1, block))
    at = (2 * GROUP - 1) * width
    write(0, (everything, slice(at, at + gmod.shape[1])), gmod[...])
    write(3, (everything, everything), gbias[...])


def swap(value, axis, bit):
    size = lax.axis_size(axis)
    return lax.ppermute(value, axis, [(i, i ^ bit) for i in range(size)])


def gather_bits(size):
    bits = [1 << b for b in range(size.bit_length() - 1)]
    return bits[1:][::-1] + bits[:1]


def dp_gather(value):
    owners = lax.axis_size("dp")
    bits = gather_bits(owners)
    held, order = value[None], [0]
    for bit in bits:
        held = jnp.concatenate([held, swap(held, "dp", bit)], axis=0)
        order = order + [o ^ bit for o in order]
    spots = [order.index(i) for i in range(owners)]
    return held, spots


def reorder(held, spots):
    return jnp.concatenate([held[s : s + 1] for s in spots], axis=0)


def group_gather(value):
    two = swap(value, "group", 2)
    one = swap(value, "group", 1)
    three = swap(two, "group", 1)
    return value, one, two, three


def dp_scatter(keep, axis, compress):
    owners = lax.axis_size("dp")
    for bit in [1 << b for b in range(owners.bit_length() - 1)]:
        shape = keep.shape
        pairs = keep.reshape(shape[:axis] + (shape[axis] // 2, 2) + shape[axis + 1 :])
        mine = lax.index_in_dim(pairs, 0, axis + 1, keepdims=False)
        theirs = lax.index_in_dim(pairs, 1, axis + 1, keepdims=False)
        if compress:
            theirs = theirs.astype(bf16)
        keep = mine + swap(theirs, "dp", bit).astype(f32)
    return lax.index_in_dim(keep, 0, axis, keepdims=False)


def reduce_blocks(keep, send):
    keep = keep + swap(send, "group", 1).astype(f32)
    keep = dp_scatter(keep, 1, True)
    sent = keep.astype(bf16)
    received = swap(sent[::-1], "group", 2)
    own = sent.astype(f32) + received.astype(f32)
    return own, swap(own, "group", 1)


def sum_all(value):
    value = value + swap(value, "group", 1)
    value = value + swap(value, "group", 2)
    owners = lax.axis_size("dp")
    for bit in [1 << b for b in range(owners.bit_length() - 1)]:
        value = value + swap(value, "dp", bit)
    return value


def compiler(limit=56):
    return pltpu.CompilerParams(
        dimension_semantics=("arbitrary",), vmem_limit_bytes=limit * 1024 * 1024
    )


def whole_spec(array):
    zeros = (0,) * len(array.shape)
    return pl.BlockSpec(tuple(array.shape), lambda l, *_: zeros)


def latent_spec(array):
    zeros = (0,) * (len(array.shape) - 1)
    return pl.BlockSpec((1,) + tuple(array.shape[1:]), lambda l, *_: (l,) + zeros)


def call(kernel, place, latent_args, whole_args, latent_outs, whole_outs, scratch, grid, flip=False):
    ins = [latent_spec(a) for a in latent_args] + [whole_spec(a) for a in whole_args]
    outs = [latent_spec(a) for a in latent_outs] + [whole_spec(a) for a in whole_outs]
    return pl.pallas_call(
        kernel,
        grid_spec=pltpu.PrefetchScalarGridSpec(
            num_scalar_prefetch=1,
            grid=(grid,),
            in_specs=ins,
            out_specs=outs,
            scratch_shapes=scratch,
        ),
        out_shape=list(latent_outs) + list(whole_outs),
        compiler_params=compiler(),
        name=kernel.__name__,
    )(place, *latent_args, *whole_args)


def like(shape, dtype):
    return jax.ShapeDtypeStruct(shape, dtype)


def body(
    latents, cotangent, timestep, labels, class_table,
    input_proj, attn_proj, mlp_down, biases,
    mean_input, mean_attn, mean_down, mean_biases,
    sq_input, sq_attn, sq_down, sq_biases,
):
    count, seq_len, width = latents.shape
    rows = input_proj.shape[0]
    owners = lax.axis_size("dp")
    hidden = mlp_down.shape[0] * owners
    heads = width // HEAD
    me = lax.axis_index("dp")
    mine = lax.axis_index("group")
    place = jnp.stack([me, mine]).astype(jnp.int32)

    class_count = class_table.shape[0]
    one_hot = (labels[:, None] == jnp.arange(class_count, dtype=jnp.int32)[None, :]).astype(bf16)
    condition = time_embed(timestep, width) + dot(one_hot, class_table)
    sigmoid_c = jax.nn.sigmoid(condition)
    cond_act = (condition * sigmoid_c).astype(bf16)
    bias_shard = biases.shape[0]
    bias_rows = -(-bias_shard // width)
    bias_b = jnp.pad(biases.astype(bf16), (0, bias_rows * width - bias_shard)).reshape(-1, width)
    small, spots = dp_gather(jnp.concatenate([cond_act, bias_b], axis=0))
    small = reorder(small, spots)
    cond_rel = small[:, :count]
    bias_rel = small[:, count:].reshape(owners, -1)[:, :bias_shard]
    absolute = jnp.arange(owners, dtype=jnp.int32) ^ me
    bias_all = jnp.take(bias_rel, absolute, axis=0).reshape(1, -1).astype(f32)
    mod_at = 3 * width + hidden
    w_mod = input_proj[:, mod_at:].astype(bf16)
    cond_cols = lax.dynamic_slice_in_dim(cond_rel.reshape(owners * count, width), me * rows, rows, 1)
    partial = dot(cond_cols, w_mod).reshape(owners, count, -1)
    bias_mod_at = 4 * width + hidden
    modulation = dp_scatter(partial, 0, False) + bias_all[:, bias_mod_at:]
    mod = modulation.reshape(count, 6, width)

    att_blocks = jnp.stack(
        [input_proj[:, b * width : (b + 1) * width] for b in range(3)] + [attn_proj]
    )
    up_blocks = jnp.stack(
        [input_proj[:, (3 + b) * width : (4 + b) * width] for b in range(hidden // width)]
    )
    down_blocks = mlp_down.reshape(GROUP, rows, width)

    def pick(blocks):
        return lax.dynamic_index_in_dim(blocks, mine, 0, keepdims=False).astype(bf16)

    def weights_of(blocks):
        held, spots = dp_gather(pick(blocks))
        return [reorder(part, spots) for part in group_gather(held)]

    att_parts = weights_of(att_blocks)
    up_parts = weights_of(up_blocks)
    down_parts = weights_of(down_blocks)

    qkv, attended, branch_a, lse = call(
        attn_forward, place,
        [latents, mod], [bias_all] + att_parts,
        [
            like((count, seq_len, 3 * width), bf16),
            like((count, seq_len, width), bf16),
            like((count, seq_len, width), f32),
            like((count, heads, seq_len), f32),
        ],
        [],
        [pltpu.VMEM((width, 4 * width), bf16), pltpu.VMEM((width, seq_len), f32)],
        count,
    )
    kept = like((2, owners, rows, width), f32)
    sent = like((2, owners, rows, width), bf16)
    bias_like = like((1, bias_mod_at), f32)
    block_out, d_middle, d_mod_m, g_attn, g_bias_m, up_keep, up_send, dn_keep, dn_send = call(
        mlp_both, place,
        [latents, cotangent, branch_a, attended, mod], [bias_all] + up_parts + down_parts,
        [
            like((count, seq_len, width), bf16),
            like((count, seq_len, width), f32),
            like((count, 6, width), f32),
        ],
        [like((width, width), f32), bias_like, kept, sent, kept, sent],
        [
            pltpu.VMEM((width, hidden), bf16),
            pltpu.VMEM((hidden, width), bf16),
            pltpu.VMEM((seq_len, hidden), bf16),
            pltpu.VMEM((seq_len, hidden), f32),
            pltpu.VMEM((seq_len, hidden), bf16),
            pltpu.VMEM((width, hidden), f32),
            pltpu.VMEM((width, hidden), f32),
        ],
        count,
    )
    grad_latents, d_mod_a, g_bias_a, at_keep, at_send = call(
        attn_backward, place,
        [latents, d_middle, qkv, lse, mod], [g_attn] + att_parts,
        [like((count, seq_len, width), f32), like((count, 2, width), f32)],
        [like((1, 2 * width), f32), kept, sent],
        [
            pltpu.VMEM((width, 4 * width), bf16),
            pltpu.VMEM((width, seq_len), f32),
            pltpu.VMEM((seq_len, 3 * width), bf16),
            pltpu.VMEM((width, 3 * width), f32),
        ],
        count,
    )

    d_modulation = jnp.concatenate([d_mod_a, d_mod_m[:, 2:]], axis=1).reshape(count, 6 * width)
    d_modulation_b = d_modulation.astype(bf16)
    bias_grad = jnp.concatenate(
        [
            g_bias_a[0],
            g_bias_m[0, 2 * width :],
            jnp.sum(d_modulation, axis=0),
        ]
    )
    dm_rel = reorder(*dp_gather(d_modulation_b))
    dm_parts = group_gather(dm_rel)
    cond_parts = group_gather(cond_rel)
    dm_all = jnp.concatenate(dm_parts, axis=0).reshape(-1, 6 * width)
    cond_all = jnp.concatenate(cond_parts, axis=0).reshape(-1, width)
    g_mod = dot(lax.dynamic_slice_in_dim(cond_all, me * rows, rows, 1), dm_all, TN)

    back = dot(dm_rel.reshape(owners * count, 6 * width), w_mod, NT).reshape(owners, count, rows)
    for bit in [1 << b for b in range(owners.bit_length() - 1)]:
        shaped = back.reshape(owners // (2 * bit), 2, bit, count, rows)
        received = swap(shaped[:, 1], "dp", bit)
        back = jnp.stack([shaped[:, 0], received], axis=1).reshape(owners, count, rows)
    back = jnp.take(back, absolute, axis=0)
    d_cond = back.transpose(1, 0, 2).reshape(count, width)
    grad_cond = d_cond * (sigmoid_c * (1.0 + condition * (1.0 - sigmoid_c)))

    up_own, up_other = reduce_blocks(up_keep, up_send)
    dn_own, dn_other = reduce_blocks(dn_keep, dn_send)
    at_own, at_other = reduce_blocks(at_keep, at_send)
    bias_sum = lax.dynamic_slice_in_dim(sum_all(bias_grad), me * bias_shard, bias_shard, 0)

    steps = rows // 16 if rows % 16 == 0 else 1
    block_rows = rows // steps

    def spec_of(array):
        if array.ndim == 3:
            return pl.BlockSpec((array.shape[0], block_rows, width), lambda s, *_: (0, s, 0))
        if array.shape[0] == 1:
            return pl.BlockSpec(tuple(array.shape), lambda s, *_: (0, 0))
        return pl.BlockSpec((block_rows, array.shape[1]), lambda s, *_: (s, 0))

    def shaped(four):
        return [four[0], four[1], four[2].reshape(GROUP, rows, width), four[3].reshape(1, -1)]

    state = (
        shaped((input_proj, attn_proj, mlp_down, biases))
        + shaped((mean_input, mean_attn, mean_down, mean_biases))
        + shaped((sq_input, sq_attn, sq_down, sq_biases))
    )
    args = [at_own, at_other, up_own, up_other, dn_own, dn_other, g_mod, bias_sum.reshape(1, -1)]
    args = args + state
    results = [like(a.shape, f32) for a in state[:4]] * 4
    outs = pl.pallas_call(
        adam_kernel,
        grid_spec=pltpu.PrefetchScalarGridSpec(
            num_scalar_prefetch=1,
            grid=(steps,),
            in_specs=[spec_of(a) for a in args],
            out_specs=[spec_of(a) for a in results],
        ),
        out_shape=results,
        compiler_params=compiler(),
        name="adam",
    )(place, *args)

    def flat(four):
        return (four[0], four[1], four[2].reshape(mlp_down.shape), four[3].reshape(-1))

    return (
        (block_out, grad_latents, grad_cond)
        + flat(outs[:4]) + flat(outs[4:8]) + flat(outs[8:12]) + flat(outs[12:16])
    )


def solution(mesh):
    tokens = P(("dp", "group"), None, None)
    four = (P("dp", None), P("dp", None), P("dp", None), P("dp"))
    in_specs = (tokens, tokens, P(("dp", "group")), P(("dp", "group")), P()) + four * 3
    out_specs = (tokens, tokens, P(("dp", "group"), None)) + four * 4
    return jax.shard_map(body, mesh=mesh, in_specs=in_specs, out_specs=out_specs, check_vma=False)
```

```python
import functools
import math

import jax
import jax.numpy as jnp
from jax import lax
from jax.experimental import pallas as pl
from jax.experimental.pallas import tpu as pltpu
from jax.sharding import PartitionSpec as P

HEAD = 64
STEP = 2
GROUP = 4

learn_rate = 0.01
beta_one = 0.9
beta_two = 0.999
adam_eps = 1e-08
norm_eps = 1e-06

f32 = jnp.float32
bf16 = jnp.bfloat16

NN = (((1,), (0,)), ((), ()))
NT = (((1,), (1,)), ((), ()))
TN = (((0,), (0,)), ((), ()))


def dot(left, right, dims=NN):
    return lax.dot_general(left, right, dims, preferred_element_type=f32)


def row_mean(values):
    return jnp.sum(values, axis=-1, keepdims=True) * (1.0 / values.shape[-1])


def layer_norm(values):
    centred = values - row_mean(values)
    inv_std = lax.rsqrt(row_mean(centred * centred) + norm_eps)
    return centred * inv_std, inv_std


def norm_back(gradient, normed, inv_std):
    return inv_std * (gradient - row_mean(gradient) - normed * row_mean(gradient * normed))


def token_sum(values):
    return jnp.sum(values, axis=0, keepdims=True)


def time_embed(timestep, model_width):
    half_width = model_width // 2
    frequency = jnp.exp(
        jnp.arange(half_width, dtype=f32) * (-math.log(10000.0) / half_width)
    )
    angles = timestep.astype(f32)[:, None] * frequency[None, :]
    return jnp.concatenate([jnp.cos(angles), jnp.sin(angles)], axis=1)


def spot_of(relative, owners):
    return (relative & 1) * (owners // 2) + (relative >> 1)


def unpack_columns(place, pieces, whole):
    owners, rows, width = pieces[0].shape
    me, mine = place[0], place[1]
    for block in range(GROUP):
        for k in range(GROUP):

            @pl.when((mine ^ k) == block)
            def _():
                for owner in range(owners):
                    whole[owner * rows : (owner + 1) * rows, block * width : (block + 1) * width] = (
                        pieces[k][spot_of(owner ^ me, owners)]
                    )


def unpack_rows(place, pieces, whole):
    owners, rows, width = pieces[0].shape
    me, mine = place[0], place[1]
    for block in range(GROUP):
        for k in range(GROUP):

            @pl.when((mine ^ k) == block)
            def _():
                for owner in range(owners):
                    start = (owner * GROUP + block) * rows
                    whole[start : start + rows, :] = pieces[k][spot_of(owner ^ me, owners)]


def pack_block(place, block, owner, value, keep, send):
    k = place[1] ^ block
    spot = spot_of(place[0] ^ owner, keep.shape[0])
    half = k >> 1

    @pl.when((k & 1) == 0)
    def _():
        keep[spot, half] = value

    @pl.when((k & 1) == 1)
    def _():
        send[spot, half] = value.astype(bf16)


def lane_masks():
    lane = lax.broadcasted_iota(jnp.int32, (1, 2 * HEAD), 1)
    low = (lane < HEAD).astype(f32)
    return low.astype(bf16), (1.0 - low).astype(bf16)


def attn_forward(place, lat, mod, bias, p0, p1, p2, p3, qkv_o, att_o, branch_o, lse_o, whole, att_t):
    width = lat.shape[-1]

    @pl.when(pl.program_id(0) == 0)
    def _():
        unpack_columns(place, (p0, p1, p2, p3), whole)

    normed, _ = layer_norm(lat[0].astype(f32))
    input_a = (normed * (1.0 + mod[0, 1:2]) + mod[0, 0:1]).astype(bf16)
    projected = dot(input_a, whole[:, : 3 * width])
    queries = (projected[:, :width] + bias[0:1, :width]).astype(bf16)
    key_vecs = projected[:, width : 2 * width].astype(bf16)
    values = (projected[:, 2 * width :] + bias[0:1, width : 2 * width]).astype(bf16)
    qkv_o[0, :, :width] = queries
    qkv_o[0, :, width : 2 * width] = key_vecs
    qkv_o[0, :, 2 * width :] = values
    values_t = values.T
    scale = 1.0 / math.sqrt(HEAD)
    masks = lane_masks()
    for pair in range(width // (2 * HEAD)):
        cols = slice(pair * 2 * HEAD, (pair + 1) * 2 * HEAD)
        for side in range(2):
            head = pair * 2 + side
            scores = dot(key_vecs[:, cols] * masks[side], queries[:, cols], NT) * scale
            peak = jnp.max(scores, axis=0, keepdims=True)
            powers = jnp.exp(scores - peak)
            total = jnp.sum(powers, axis=0, keepdims=True)
            lse_o[0, head : head + 1, :] = peak + jnp.log(total)
            probs = (powers * (1.0 / total)).astype(bf16)
            att_t[head * HEAD : (head + 1) * HEAD, :] = dot(
                values_t[head * HEAD : (head + 1) * HEAD, :], probs
            )
    attended = att_t[...].T.astype(bf16)
    att_o[0] = attended
    branch_o[0] = dot(attended, whole[:, 3 * width :]) + bias[0:1, 2 * width : 3 * width]


def mlp_both(
    place, lat, cot, branch, att, mod, bias,
    u0, u1, u2, u3, w0, w1, w2, w3,
    out_o, dmid_o, dmod_o, gattn_o, gbias_o, upk_o, ups_o, dnk_o, dns_o,
    w_up, w_down, gelu_s, slope_s, dpre_s, acc_up, acc_down,
):
    width = lat.shape[-1]
    hidden = w_up.shape[1]
    step = pl.program_id(0)
    first = step == 0

    @pl.when(first)
    def _():
        unpack_columns(place, (u0, u1, u2, u3), w_up)
        unpack_rows(place, (w0, w1, w2, w3), w_down)
        acc_up[...] = jnp.zeros_like(acc_up)
        acc_down[...] = jnp.zeros_like(acc_down)
        gattn_o[...] = jnp.zeros_like(gattn_o)
        gbias_o[...] = jnp.zeros_like(gbias_o)

    b_up = bias[0:1, 3 * width : 3 * width + hidden]
    b_down = bias[0:1, 3 * width + hidden : 4 * width + hidden]
    gate_a, shift_m, scale_m, gate_m = mod[0, 2:3], mod[0, 3:4], mod[0, 4:5], mod[0, 5:6]
    branch_a = branch[0]
    middle = lat[0].astype(f32) + gate_a * branch_a
    normed, inv_std = layer_norm(middle)
    input_m = (normed * (1.0 + scale_m) + shift_m).astype(bf16)
    inner = math.sqrt(2.0 / math.pi)
    chunk = 512
    for start in range(0, hidden, chunk):
        cols = slice(start, start + chunk)
        pre = dot(input_m, w_up[:, cols]) + b_up[:, cols]
        square = pre * pre
        tangent = jnp.tanh(pre * (inner + (inner * 0.044715) * square))
        upper = 0.5 * (1.0 + tangent)
        gelu_s[:, cols] = (pre * upper).astype(bf16)
        slope_s[:, cols] = upper + (0.5 * pre) * (1.0 - tangent * tangent) * (
            inner + (inner * 3.0 * 0.044715) * square
        )
    branch_m = dot(gelu_s[...], w_down[...]) + b_down
    out_o[0] = (middle + gate_m * branch_m).astype(bf16)
    grad_out = cot[0].astype(f32)
    dmod_o[0, 5:6] = token_sum(grad_out * branch_m)
    d_branch_m = grad_out * gate_m
    d_branch_mb = d_branch_m.astype(bf16)
    acc_down[...] += dot(d_branch_mb, gelu_s[...], TN)
    gbias_o[0:1, 3 * width + hidden : 4 * width + hidden] += token_sum(d_branch_m)
    for start in range(0, hidden, chunk):
        cols = slice(start, start + chunk)
        d_pre = dot(d_branch_mb, w_down[cols, :], NT) * slope_s[:, cols]
        gbias_o[0:1, 3 * width + start : 3 * width + start + chunk] += token_sum(d_pre)
        dpre_s[:, cols] = d_pre.astype(bf16)
    acc_up[...] += dot(input_m, dpre_s[...], TN)
    d_input = dot(dpre_s[...], w_up[...], NT)
    dmod_o[0, 4:5] = token_sum(d_input * normed)
    dmod_o[0, 3:4] = token_sum(d_input)
    d_middle = grad_out + norm_back(d_input * (1.0 + scale_m), normed, inv_std)
    dmid_o[0] = d_middle
    dmod_o[0, 2:3] = token_sum(d_middle * branch_a)
    d_branch_a = d_middle * gate_a
    gbias_o[0:1, 2 * width : 3 * width] += token_sum(d_branch_a)
    gattn_o[...] += dot(att[0], d_branch_a.astype(bf16), TN)

    @pl.when(step == pl.num_programs(0) - 1)
    def _():
        owners, rows = upk_o.shape[0], upk_o.shape[2]
        for block in range(GROUP):
            for owner in range(owners):
                value = acc_up[owner * rows : (owner + 1) * rows, block * width : (block + 1) * width]
                pack_block(place, block, owner, value, upk_o, ups_o)
        whole_down = acc_down[...].T
        for block in range(GROUP):
            for owner in range(owners):
                start = (owner * GROUP + block) * rows
                pack_block(place, block, owner, whole_down[start : start + rows, :], dnk_o, dns_o)


def attn_backward(first, last, place, lat, dmid, qkv, lse, mod, p0, p1, p2, p3, *refs):
    refs = list(refs)
    if not first:
        acc_i, gbias_i = refs.pop(0), refs.pop(0)
    if last:
        gattn = refs.pop(0)
    glat_o, dmod_o, gbias_o = refs.pop(0), refs.pop(0), refs.pop(0)
    if last:
        keep_o, send_o, whole, dq_t, dproj, acc = refs
    else:
        acc, whole, dq_t, dproj = refs
    width = lat.shape[-1]
    step = pl.program_id(0)

    @pl.when(step == 0)
    def _():
        unpack_columns(place, (p0, p1, p2, p3), whole)
        acc[...] = jnp.zeros_like(acc) if first else acc_i[...]
        gbias_o[...] = jnp.zeros_like(gbias_o) if first else gbias_i[...]

    shift_a, scale_a, gate_a = mod[0, 0:1], mod[0, 1:2], mod[0, 2:3]
    normed, inv_std = layer_norm(lat[0].astype(f32))
    input_a = (normed * (1.0 + scale_a) + shift_a).astype(bf16)
    d_middle = dmid[0]
    d_att = dot((d_middle * gate_a).astype(bf16), whole[:, 3 * width :], NT).astype(bf16)
    scale = 1.0 / math.sqrt(HEAD)
    masks = lane_masks()
    low = lax.broadcasted_iota(jnp.int32, (1, 2 * HEAD), 1) < HEAD
    keys_t = qkv[0, :, width : 2 * width].T
    for pair in range(width // (2 * HEAD)):
        cols = slice(pair * 2 * HEAD, (pair + 1) * 2 * HEAD)
        q_pair = qkv[0, :, pair * 2 * HEAD : (pair + 1) * 2 * HEAD]
        k_pair = qkv[0, :, width + pair * 2 * HEAD : width + (pair + 1) * 2 * HEAD]
        v_pair = qkv[0, :, 2 * width + pair * 2 * HEAD : 2 * width + (pair + 1) * 2 * HEAD]
        do_pair = d_att[:, cols]
        d_keys, d_values = [], []
        for side in range(2):
            head = pair * 2 + side
            scores = dot(k_pair * masks[side], q_pair, NT) * scale
            probs = jnp.exp(scores - lse[0, head : head + 1, :])
            d_values.append(dot(probs.astype(bf16), do_pair))
            d_probs = dot(v_pair * masks[side], do_pair, NT)
            delta = jnp.sum(probs * d_probs, axis=0, keepdims=True)
            d_scores = (probs * (d_probs - delta) * scale).astype(bf16)
            d_keys.append(dot(d_scores, q_pair))
            dq_t[head * HEAD : (head + 1) * HEAD, :] = dot(
                keys_t[head * HEAD : (head + 1) * HEAD, :], d_scores
            )
        d_key = jnp.where(low, d_keys[0], d_keys[1])
        d_value = jnp.where(low, d_values[0], d_values[1])
        dproj[:, width + pair * 2 * HEAD : width + (pair + 1) * 2 * HEAD] = d_key.astype(bf16)
        dproj[:, 2 * width + pair * 2 * HEAD : 2 * width + (pair + 1) * 2 * HEAD] = d_value.astype(
            bf16
        )
        gbias_o[0:1, width + pair * 2 * HEAD : width + (pair + 1) * 2 * HEAD] += token_sum(d_value)
    d_query = dq_t[...].T
    gbias_o[0:1, :width] += token_sum(d_query)
    dproj[:, :width] = d_query.astype(bf16)
    acc[...] += dot(input_a, dproj[...], TN)
    d_input = dot(dproj[...], whole[:, : 3 * width], NT)
    dmod_o[0, 1:2] = token_sum(d_input * normed)
    dmod_o[0, 0:1] = token_sum(d_input)
    glat_o[0] = d_middle + norm_back(d_input * (1.0 + scale_a), normed, inv_std)

    if last:

        @pl.when(step == pl.num_programs(0) - 1)
        def _():
            owners, rows = keep_o.shape[0], keep_o.shape[2]
            for block in range(GROUP):
                for owner in range(owners):
                    span = slice(owner * rows, (owner + 1) * rows)
                    if block < GROUP - 1:
                        value = acc[span, block * width : (block + 1) * width]
                    else:
                        value = gattn[span, :]
                    pack_block(place, block, owner, value, keep_o, send_o)


def adam_parts(weight, moment, second, gradient):
    moment = beta_one * moment + (1.0 - beta_one) * gradient
    second = beta_two * second + (1.0 - beta_two) * gradient * gradient
    first_fix = 1.0 - beta_one**STEP
    second_fix = 1.0 - beta_two**STEP
    weight = weight - (learn_rate / first_fix) * moment / (
        jnp.sqrt(second * (1.0 / second_fix)) + adam_eps
    )
    return weight, moment, second


def adam_kernel(place, *refs):
    att, up, down, gmod = refs[0:4], refs[4:8], refs[8:12], refs[12]
    weights, means, squares = refs[13:16], refs[16:19], refs[19:22]
    grads, new_w, new_m, new_s = refs[22:25], refs[25:28], refs[28:31], refs[31:34]
    width = att[0].shape[-1]

    def write(which, where, gradient):
        grads[which][where] = gradient
        result = adam_parts(
            weights[which][where], means[which][where], squares[which][where], gradient
        )
        new_w[which][where], new_m[which][where], new_s[which][where] = result

    def block_of(parts, block):
        k = place[1] ^ block
        half = k >> 1
        near = parts[0][half].astype(f32) + parts[1][1 - half].astype(f32)
        far = parts[2][half].astype(f32) + parts[3][1 - half].astype(f32)
        return jnp.where((k & 1) == 0, near, far)

    everything = slice(None)
    for block in range(GROUP):
        g_att = block_of(att, block)
        if block < GROUP - 1:
            write(0, (everything, slice(block * width, (block + 1) * width)), g_att)
        else:
            write(1, (everything, everything), g_att)
        at = (GROUP - 1 + block) * width
        write(0, (everything, slice(at, at + width)), block_of(up, block))
        write(2, (block,), block_of(down, block))
    at = (2 * GROUP - 1) * width
    write(0, (everything, slice(at, at + gmod.shape[1])), gmod[...])


def swap(value, axis, bit):
    size = lax.axis_size(axis)
    return lax.ppermute(value, axis, [(i, i ^ bit) for i in range(size)])


def upper_stages(owners):
    half = owners // 2
    if half <= 4:
        return [list(range(1, half))]
    return [[1 << b] for b in range(half.bit_length() - 1)]


def gather_upper(held):
    for stage in upper_stages(lax.axis_size("dp")):
        held = jnp.concatenate([held] + [swap(held, "dp", 2 * c) for c in stage], axis=0)
    return held


def dp_gather(value):
    held = gather_upper(value[None])
    return jnp.concatenate([held, swap(held, "dp", 1)], axis=0)


def group_gather(value):
    two = swap(value, "group", 2)
    one = swap(value, "group", 1)
    three = swap(two, "group", 1)
    return value, one, two, three


def scatter_near(keep, dtype):
    half = keep.shape[0] // 2
    return keep[:half] + swap(keep[half:].astype(dtype), "dp", 1).astype(f32)


def scatter_upper(keep, dtype):
    for stage in upper_stages(lax.axis_size("dp")):
        if len(stage) == keep.shape[0] - 1:
            total = keep[0]
            for c in stage:
                total = total + swap(keep[c].astype(dtype), "dp", 2 * c).astype(f32)
            return total
        bit = stage[0]
        pairs = keep.reshape((keep.shape[0] // 2, 2) + keep.shape[1:])
        keep = pairs[:, 0] + swap(pairs[:, 1].astype(dtype), "dp", 2 * bit).astype(f32)
    return keep[0]


def share_parts(total):
    sent = total.astype(bf16)
    return [sent] + [swap(sent, "group", k) for k in (2, 1, 3)]


def sum_all(value):
    value = value + swap(value, "group", 1)
    value = value + swap(value, "group", 2)
    owners = lax.axis_size("dp")
    for bit in [1 << b for b in range(owners.bit_length() - 1)]:
        value = value + swap(value, "dp", bit)
    return value


def compiler(limit=56):
    return pltpu.CompilerParams(
        dimension_semantics=("arbitrary",), vmem_limit_bytes=limit * 1024 * 1024
    )


def whole_spec(array):
    zeros = (0,) * len(array.shape)
    return pl.BlockSpec(tuple(array.shape), lambda l, *_: zeros)


def latent_spec(array):
    zeros = (0,) * (len(array.shape) - 1)
    return pl.BlockSpec((1,) + tuple(array.shape[1:]), lambda l, *_: (l,) + zeros)


def call(kernel, place, latent_args, whole_args, latent_outs, whole_outs, scratch, grid, start=0, us=15):
    def shifted(array):
        zeros = (0,) * (len(array.shape) - 1)
        return pl.BlockSpec((1,) + tuple(array.shape[1:]), lambda l, *_: (l + start,) + zeros)

    ins = [shifted(a) for a in latent_args] + [whole_spec(a) for a in whole_args]
    outs = [latent_spec(a) for a in latent_outs] + [whole_spec(a) for a in whole_outs]
    func = kernel.func if isinstance(kernel, functools.partial) else kernel
    return pl.pallas_call(
        kernel,
        grid_spec=pltpu.PrefetchScalarGridSpec(
            num_scalar_prefetch=1,
            grid=(grid,),
            in_specs=ins,
            out_specs=outs,
            scratch_shapes=scratch,
        ),
        out_shape=list(latent_outs) + list(whole_outs),
        compiler_params=compiler(),
        cost_estimate=pl.CostEstimate(
            flops=int(us * 1e9), bytes_accessed=int(us * 1e6), transcendentals=0
        ),
        name=func.__name__,
    )(place, *latent_args, *whole_args)


def like(shape, dtype):
    return jax.ShapeDtypeStruct(shape, dtype)


def body(
    latents, cotangent, timestep, labels, class_table,
    input_proj, attn_proj, mlp_down, biases,
    mean_input, mean_attn, mean_down, mean_biases,
    sq_input, sq_attn, sq_down, sq_biases,
):
    count, seq_len, width = latents.shape
    rows = input_proj.shape[0]
    owners = lax.axis_size("dp")
    hidden = mlp_down.shape[0] * owners
    heads = width // HEAD
    me = lax.axis_index("dp")
    mine = lax.axis_index("group")
    place = jnp.stack([me, mine]).astype(jnp.int32)

    bias_shard = biases.shape[0]
    message = jnp.concatenate([timestep.astype(f32), labels.astype(f32), biases])
    small = dp_gather(message)
    times_rel = small[:, :count].reshape(-1)
    labels_rel = small[:, count : 2 * count].reshape(-1).astype(jnp.int32)
    absolute = spot_of(jnp.arange(owners, dtype=jnp.int32) ^ me, owners)
    bias_all = (
        jnp.take(small[:, 2 * count :], absolute, axis=0).reshape(1, -1).astype(bf16).astype(f32)
    )
    class_count = class_table.shape[0]
    one_hot = (labels_rel[:, None] == jnp.arange(class_count, dtype=jnp.int32)[None, :]).astype(bf16)
    condition = time_embed(times_rel, width) + dot(one_hot, class_table)
    cond_rel = (condition * jax.nn.sigmoid(condition)).astype(bf16)
    mod_at = 3 * width + hidden
    w_mod = input_proj[:, mod_at:].astype(bf16)
    cond_cols = lax.dynamic_slice_in_dim(cond_rel, me * rows, rows, 1)
    partial = dot(cond_cols, w_mod).reshape(owners, count, -1)
    bias_mod_at = 4 * width + hidden
    modulation = scatter_upper(scatter_near(partial, f32), f32) + bias_all[:, bias_mod_at:]
    mod = modulation.reshape(count, 6, width)

    att_blocks = [input_proj[:, b * width : (b + 1) * width] for b in range(3)] + [attn_proj]
    up_blocks = [input_proj[:, (3 + b) * width : (4 + b) * width] for b in range(GROUP)]
    down_blocks = [mlp_down[b * rows : (b + 1) * rows] for b in range(GROUP)]

    def weights_of(blocks):
        chosen = jnp.where(
            mine < 2,
            jnp.where(mine == 0, blocks[0], blocks[1]),
            jnp.where(mine == 2, blocks[2], blocks[3]),
        ).astype(bf16)
        return list(group_gather(dp_gather(chosen)))

    att_parts = weights_of(att_blocks)
    up_parts = weights_of(up_blocks)
    down_parts = weights_of(down_blocks)

    qkv, attended, branch_a, lse = call(
        attn_forward, place,
        [latents, mod], [bias_all] + att_parts,
        [
            like((count, seq_len, 3 * width), bf16),
            like((count, seq_len, width), bf16),
            like((count, seq_len, width), f32),
            like((count, heads, seq_len), f32),
        ],
        [],
        [pltpu.VMEM((width, 4 * width), bf16), pltpu.VMEM((width, seq_len), f32)],
        count,
    )
    kept = like((owners, 2, rows, width), f32)
    sent = like((owners, 2, rows, width), bf16)
    bias_like = like((1, bias_mod_at), f32)
    block_out, d_middle, d_mod_m, g_attn, g_bias_m, up_keep, up_send, dn_keep, dn_send = call(
        mlp_both, place,
        [latents, cotangent, branch_a, attended, mod], [bias_all] + up_parts + down_parts,
        [
            like((count, seq_len, width), bf16),
            like((count, seq_len, width), f32),
            like((count, 6, width), f32),
        ],
        [like((width, width), f32), bias_like, kept, sent, kept, sent],
        [
            pltpu.VMEM((width, hidden), bf16),
            pltpu.VMEM((hidden, width), bf16),
            pltpu.VMEM((seq_len, hidden), bf16),
            pltpu.VMEM((seq_len, hidden), f32),
            pltpu.VMEM((seq_len, hidden), bf16),
            pltpu.VMEM((width, hidden), f32),
            pltpu.VMEM((width, hidden), f32),
        ],
        count,
        us=20,
    )
    up_keep = up_keep + swap(up_send, "group", 1).astype(f32)
    dn_keep = dn_keep + swap(dn_send, "group", 1).astype(f32)
    d_middle, up_keep, dn_keep = lax.optimization_barrier((d_middle, up_keep, dn_keep))

    half = count // 2
    token_like = like((half, seq_len, width), f32)
    mod_like = like((half, 2, width), f32)
    gb_like = like((1, 2 * width), f32)
    acc_like = like((width, 3 * width), f32)
    scratch = [
        pltpu.VMEM((width, 4 * width), bf16),
        pltpu.VMEM((width, seq_len), f32),
        pltpu.VMEM((seq_len, 3 * width), bf16),
    ]
    token_args = [latents, d_middle, qkv, lse, mod]
    glat_0, d_mod_0, g_bias_a, acc = call(
        functools.partial(attn_backward, True, False), place,
        token_args, att_parts,
        [token_like, mod_like], [gb_like, acc_like], scratch, half, 0, 10,
    )
    up_keep = scatter_near(up_keep, bf16)
    dn_keep = scatter_near(dn_keep, bf16)
    acc, up_keep, dn_keep = lax.optimization_barrier((acc, up_keep, dn_keep))
    glat_1, d_mod_1, g_bias_a, at_keep, at_send = call(
        functools.partial(attn_backward, False, True), place,
        token_args, att_parts + [acc, g_bias_a, g_attn],
        [token_like, mod_like], [gb_like, kept, sent],
        scratch + [pltpu.VMEM((width, 3 * width), f32)], count - half, half, 10,
    )
    up_total = scatter_upper(up_keep, bf16)
    dn_total = scatter_upper(dn_keep, bf16)
    at_send, up_total, dn_total = lax.optimization_barrier((at_send, up_total, dn_total))
    at_keep = at_keep + swap(at_send, "group", 1).astype(f32)
    at_total = scatter_upper(scatter_near(at_keep, bf16), bf16)
    grad_latents = jnp.concatenate([glat_0, glat_1], axis=0)

    d_mod_a = jnp.concatenate([d_mod_0, d_mod_1], axis=0)
    d_modulation = jnp.concatenate([d_mod_a, d_mod_m[:, 2:]], axis=1).reshape(count, 6 * width)
    d_modulation_b = d_modulation.astype(bf16)
    bias_grad = jnp.concatenate(
        [
            g_bias_a[0],
            g_bias_m[0, 2 * width :],
            jnp.sum(d_modulation, axis=0),
        ]
    )
    dm_rel = dp_gather(d_modulation_b).reshape(owners * count, 6 * width)
    dm_all = jnp.concatenate(group_gather(dm_rel), axis=0)
    cond_all = jnp.concatenate(group_gather(cond_cols), axis=0)
    g_mod = dot(cond_all, dm_all, TN)

    back = dp_gather(dot(dm_rel, w_mod, NT))
    back = back.reshape(owners, owners, count, rows)
    back = jnp.stack([back[s, s] for s in range(owners)])
    back = jnp.take(back, absolute, axis=0)
    d_cond = back.transpose(1, 0, 2).reshape(count, width)
    own_cond = condition[:count]
    own_sig = jax.nn.sigmoid(own_cond)
    grad_cond = d_cond * (own_sig * (1.0 + own_cond * (1.0 - own_sig)))

    parts = share_parts(at_total) + share_parts(up_total) + share_parts(dn_total)
    g_biases = lax.dynamic_slice_in_dim(sum_all(bias_grad), me * bias_shard, bias_shard, 0)
    bias_out = (g_biases,) + adam_parts(biases, mean_biases, sq_biases, g_biases)

    steps = rows // 16 if rows % 16 == 0 else 1
    block_rows = rows // steps

    def spec_of(array):
        if len(array.shape) == 3:
            return pl.BlockSpec((array.shape[0], block_rows, width), lambda s, *_: (0, s, 0))
        return pl.BlockSpec((block_rows, array.shape[1]), lambda s, *_: (s, 0))

    state = [
        entry
        for three in (
            (input_proj, attn_proj, mlp_down),
            (mean_input, mean_attn, mean_down),
            (sq_input, sq_attn, sq_down),
        )
        for entry in (three[0], three[1], three[2].reshape(GROUP, rows, width))
    ]
    args = parts + [g_mod] + state
    results = [like(a.shape, f32) for a in state[:3]] * 4
    outs = pl.pallas_call(
        adam_kernel,
        grid_spec=pltpu.PrefetchScalarGridSpec(
            num_scalar_prefetch=1,
            grid=(steps,),
            in_specs=[spec_of(a) for a in args],
            out_specs=[spec_of(a) for a in results],
        ),
        out_shape=results,
        compiler_params=compiler(),
        name="adam",
    )(place, *args)

    def flat(index):
        three = outs[3 * index : 3 * index + 3]
        return (three[0], three[1], three[2].reshape(mlp_down.shape), bias_out[index])

    return (block_out, grad_latents, grad_cond) + flat(0) + flat(1) + flat(2) + flat(3)


def solution(mesh):
    tokens = P(("dp", "group"), None, None)
    four = (P("dp", None), P("dp", None), P("dp", None), P("dp"))
    in_specs = (tokens, tokens, P(("dp", "group")), P(("dp", "group")), P()) + four * 3
    out_specs = (tokens, tokens, P(("dp", "group"), None)) + four * 4
    return jax.shard_map(body, mesh=mesh, in_specs=in_specs, out_specs=out_specs, check_vma=False)
```

```python
import functools
import math

import jax
import jax.numpy as jnp
from jax import lax
from jax.experimental import pallas as pl
from jax.experimental.pallas import tpu as pltpu
from jax.sharding import PartitionSpec as P

HEAD = 64
STEP = 2
GROUP = 4

learn_rate = 0.01
beta_one = 0.9
beta_two = 0.999
adam_eps = 1e-08
norm_eps = 1e-06

f32 = jnp.float32
bf16 = jnp.bfloat16

NN = (((1,), (0,)), ((), ()))
NT = (((1,), (1,)), ((), ()))
TN = (((0,), (0,)), ((), ()))


def dot(left, right, dims=NN):
    return lax.dot_general(left, right, dims, preferred_element_type=f32)


def row_mean(values):
    return jnp.sum(values, axis=-1, keepdims=True) * (1.0 / values.shape[-1])


def layer_norm(values):
    centred = values - row_mean(values)
    inv_std = lax.rsqrt(row_mean(centred * centred) + norm_eps)
    return centred * inv_std, inv_std


def norm_back(gradient, normed, inv_std):
    return inv_std * (gradient - row_mean(gradient) - normed * row_mean(gradient * normed))


def token_sum(values):
    return jnp.sum(values, axis=0, keepdims=True)


def time_embed(timestep, model_width):
    half_width = model_width // 2
    frequency = jnp.exp(
        jnp.arange(half_width, dtype=f32) * (-math.log(10000.0) / half_width)
    )
    angles = timestep.astype(f32)[:, None] * frequency[None, :]
    return jnp.concatenate([jnp.cos(angles), jnp.sin(angles)], axis=1)


def spot_of(relative, owners):
    return (relative & 1) * (owners // 2) + (relative >> 1)


def unpack_attn(place, own, other, whole):
    owners, width = own.shape[0], own.shape[-1]
    rows = whole.shape[0] // owners
    for core in range(2):
        for source, near in ((own, True), (other, False)):

            @pl.when(((place[1] & 1) == core) == near)
            def _():
                for part in range(2):
                    block = 2 * core + part
                    for owner in range(owners):
                        whole[
                            owner * rows : (owner + 1) * rows, block * width : (block + 1) * width
                        ] = source[owner, part * rows : (part + 1) * rows, :]


def unpack_mlp(place, own, other, w_up, w_down):
    width = w_up.shape[0]
    upper = own[0].shape[0]
    owners = 2 * upper
    rows = width // owners
    for core in range(2):
        for source, near in ((own, True), (other, False)):
            for side in range(2):

                @pl.when((((place[1] & 1) == core) == near))
                def _():
                    for owner in range(owners):

                        @pl.when(((place[0] ^ owner) & 1) == side)
                        def _():
                            spot = (place[0] ^ owner) >> 1
                            piece = source[side]
                            for part in range(2):
                                block = 2 * core + part
                                w_up[
                                    owner * rows : (owner + 1) * rows,
                                    block * width : (block + 1) * width,
                                ] = piece[spot, part * rows : (part + 1) * rows, :]
                            start = (owner * GROUP + 2 * core) * rows
                            w_down[start : start + 2 * rows, :] = piece[spot, 2 * rows : 4 * rows, :]


def pack_block(place, block, spot, value, keep, send, offset=0):
    k = place[1] ^ block
    half = (k >> 1) + offset

    @pl.when((k & 1) == 0)
    def _():
        keep[spot, half] = value

    @pl.when((k & 1) == 1)
    def _():
        send[spot, half] = value.astype(bf16)


def lane_masks():
    lane = lax.broadcasted_iota(jnp.int32, (1, 2 * HEAD), 1)
    low = (lane < HEAD).astype(f32)
    return low.astype(bf16), (1.0 - low).astype(bf16)


def attn_forward(place, lat, mod, bias, own, other, qkv_o, att_o, branch_o, lse_o, whole, att_t):
    width = lat.shape[-1]

    @pl.when(pl.program_id(0) == 0)
    def _():
        unpack_attn(place, own, other, whole)

    normed, _ = layer_norm(lat[0].astype(f32))
    input_a = (normed * (1.0 + mod[0, 1:2]) + mod[0, 0:1]).astype(bf16)
    projected = dot(input_a, whole[:, : 3 * width])
    queries = (projected[:, :width] + bias[0:1, :width]).astype(bf16)
    key_vecs = projected[:, width : 2 * width].astype(bf16)
    values = (projected[:, 2 * width :] + bias[0:1, width : 2 * width]).astype(bf16)
    qkv_o[0, :, :width] = queries
    qkv_o[0, :, width : 2 * width] = key_vecs
    qkv_o[0, :, 2 * width :] = values
    values_t = values.T
    scale = 1.0 / math.sqrt(HEAD)
    masks = lane_masks()
    for pair in range(width // (2 * HEAD)):
        cols = slice(pair * 2 * HEAD, (pair + 1) * 2 * HEAD)
        for side in range(2):
            head = pair * 2 + side
            scores = dot(key_vecs[:, cols] * masks[side], queries[:, cols], NT) * scale
            peak = jnp.max(scores, axis=0, keepdims=True)
            powers = jnp.exp(scores - peak)
            total = jnp.sum(powers, axis=0, keepdims=True)
            lse_o[0, head : head + 1, :] = peak + jnp.log(total)
            probs = (powers * (1.0 / total)).astype(bf16)
            att_t[head * HEAD : (head + 1) * HEAD, :] = dot(
                values_t[head * HEAD : (head + 1) * HEAD, :], probs
            )
    attended = att_t[...].T.astype(bf16)
    att_o[0] = attended
    branch_o[0] = dot(attended, whole[:, 3 * width :]) + bias[0:1, 2 * width : 3 * width]


def mlp_both(
    place, lat, cot, branch, att, mod, bias,
    own_near, own_far, other_near, other_far,
    out_o, dmid_o, dmod_o, gattn_o, gbias_o, keep_o, send_o,
    w_up, w_down, gelu_s, slope_s, dpre_s, acc_up, acc_down,
):
    width = lat.shape[-1]
    hidden = w_up.shape[1]
    step = pl.program_id(0)
    first = step == 0

    @pl.when(first)
    def _():
        unpack_mlp(place, (own_near, own_far), (other_near, other_far), w_up, w_down)
        acc_up[...] = jnp.zeros_like(acc_up)
        acc_down[...] = jnp.zeros_like(acc_down)
        gattn_o[...] = jnp.zeros_like(gattn_o)
        gbias_o[...] = jnp.zeros_like(gbias_o)

    b_up = bias[0:1, 3 * width : 3 * width + hidden]
    b_down = bias[0:1, 3 * width + hidden : 4 * width + hidden]
    gate_a, shift_m, scale_m, gate_m = mod[0, 2:3], mod[0, 3:4], mod[0, 4:5], mod[0, 5:6]
    branch_a = branch[0]
    middle = lat[0].astype(f32) + gate_a * branch_a
    normed, inv_std = layer_norm(middle)
    input_m = (normed * (1.0 + scale_m) + shift_m).astype(bf16)
    inner = math.sqrt(2.0 / math.pi)
    chunk = 512
    for start in range(0, hidden, chunk):
        cols = slice(start, start + chunk)
        pre = dot(input_m, w_up[:, cols]) + b_up[:, cols]
        square = pre * pre
        tangent = jnp.tanh(pre * (inner + (inner * 0.044715) * square))
        upper = 0.5 * (1.0 + tangent)
        gelu_s[:, cols] = (pre * upper).astype(bf16)
        slope_s[:, cols] = upper + (0.5 * pre) * (1.0 - tangent * tangent) * (
            inner + (inner * 3.0 * 0.044715) * square
        )
    branch_m = dot(gelu_s[...], w_down[...]) + b_down
    out_o[0] = (middle + gate_m * branch_m).astype(bf16)
    grad_out = cot[0].astype(f32)
    dmod_o[0, 5:6] = token_sum(grad_out * branch_m)
    d_branch_m = grad_out * gate_m
    d_branch_mb = d_branch_m.astype(bf16)
    acc_down[...] += dot(d_branch_mb, gelu_s[...], TN)
    gbias_o[0:1, 3 * width + hidden : 4 * width + hidden] += token_sum(d_branch_m)
    for start in range(0, hidden, chunk):
        cols = slice(start, start + chunk)
        d_pre = dot(d_branch_mb, w_down[cols, :], NT) * slope_s[:, cols]
        gbias_o[0:1, 3 * width + start : 3 * width + start + chunk] += token_sum(d_pre)
        dpre_s[:, cols] = d_pre.astype(bf16)
    acc_up[...] += dot(input_m, dpre_s[...], TN)
    d_input = dot(dpre_s[...], w_up[...], NT)
    dmod_o[0, 4:5] = token_sum(d_input * normed)
    dmod_o[0, 3:4] = token_sum(d_input)
    d_middle = grad_out + norm_back(d_input * (1.0 + scale_m), normed, inv_std)
    dmid_o[0] = d_middle
    dmod_o[0, 2:3] = token_sum(d_middle * branch_a)
    d_branch_a = d_middle * gate_a
    gbias_o[0:1, 2 * width : 3 * width] += token_sum(d_branch_a)
    gattn_o[...] += dot(att[0], d_branch_a.astype(bf16), TN)

    @pl.when(step == pl.num_programs(0) - 1)
    def _():
        owners, rows = keep_o.shape[0], keep_o.shape[2]
        whole_down = acc_down[...].T
        for owner in range(owners):
            spot = spot_of(place[0] ^ owner, owners)
            for block in range(GROUP):
                value = acc_up[owner * rows : (owner + 1) * rows, block * width : (block + 1) * width]
                pack_block(place, block, spot, value, keep_o, send_o)
                start = (owner * GROUP + block) * rows
                value = whole_down[start : start + rows, :]
                pack_block(place, block, spot, value, keep_o, send_o, 2)


def attn_backward(first, last, place, lat, dmid, qkv, lse, mod, own, other, *refs):
    refs = list(refs)
    if not first:
        acc_i, gbias_i = refs.pop(0), refs.pop(0)
    if last:
        gattn = refs.pop(0)
    glat_o, dmod_o, gbias_o = refs.pop(0), refs.pop(0), refs.pop(0)
    if last:
        keep_o, send_o, whole, dq_t, dproj, acc = refs
    else:
        acc, whole, dq_t, dproj = refs
    width = lat.shape[-1]
    step = pl.program_id(0)

    @pl.when(step == 0)
    def _():
        unpack_attn(place, own, other, whole)
        acc[...] = jnp.zeros_like(acc) if first else acc_i[...]
        gbias_o[...] = jnp.zeros_like(gbias_o) if first else gbias_i[...]

    shift_a, scale_a, gate_a = mod[0, 0:1], mod[0, 1:2], mod[0, 2:3]
    normed, inv_std = layer_norm(lat[0].astype(f32))
    input_a = (normed * (1.0 + scale_a) + shift_a).astype(bf16)
    d_middle = dmid[0]
    d_att = dot((d_middle * gate_a).astype(bf16), whole[:, 3 * width :], NT).astype(bf16)
    scale = 1.0 / math.sqrt(HEAD)
    masks = lane_masks()
    low = lax.broadcasted_iota(jnp.int32, (1, 2 * HEAD), 1) < HEAD
    keys_t = qkv[0, :, width : 2 * width].T
    for pair in range(width // (2 * HEAD)):
        cols = slice(pair * 2 * HEAD, (pair + 1) * 2 * HEAD)
        q_pair = qkv[0, :, pair * 2 * HEAD : (pair + 1) * 2 * HEAD]
        k_pair = qkv[0, :, width + pair * 2 * HEAD : width + (pair + 1) * 2 * HEAD]
        v_pair = qkv[0, :, 2 * width + pair * 2 * HEAD : 2 * width + (pair + 1) * 2 * HEAD]
        do_pair = d_att[:, cols]
        d_keys, d_values = [], []
        for side in range(2):
            head = pair * 2 + side
            scores = dot(k_pair * masks[side], q_pair, NT) * scale
            probs = jnp.exp(scores - lse[0, head : head + 1, :])
            d_values.append(dot(probs.astype(bf16), do_pair))
            d_probs = dot(v_pair * masks[side], do_pair, NT)
            delta = jnp.sum(probs * d_probs, axis=0, keepdims=True)
            d_scores = (probs * (d_probs - delta) * scale).astype(bf16)
            d_keys.append(dot(d_scores, q_pair))
            dq_t[head * HEAD : (head + 1) * HEAD, :] = dot(
                keys_t[head * HEAD : (head + 1) * HEAD, :], d_scores
            )
        d_key = jnp.where(low, d_keys[0], d_keys[1])
        d_value = jnp.where(low, d_values[0], d_values[1])
        dproj[:, width + pair * 2 * HEAD : width + (pair + 1) * 2 * HEAD] = d_key.astype(bf16)
        dproj[:, 2 * width + pair * 2 * HEAD : 2 * width + (pair + 1) * 2 * HEAD] = d_value.astype(
            bf16
        )
        gbias_o[0:1, width + pair * 2 * HEAD : width + (pair + 1) * 2 * HEAD] += token_sum(d_value)
    d_query = dq_t[...].T
    gbias_o[0:1, :width] += token_sum(d_query)
    dproj[:, :width] = d_query.astype(bf16)
    acc[...] += dot(input_a, dproj[...], TN)
    d_input = dot(dproj[...], whole[:, : 3 * width], NT)
    dmod_o[0, 1:2] = token_sum(d_input * normed)
    dmod_o[0, 0:1] = token_sum(d_input)
    glat_o[0] = d_middle + norm_back(d_input * (1.0 + scale_a), normed, inv_std)

    if last:

        @pl.when(step == pl.num_programs(0) - 1)
        def _():
            owners, rows = keep_o.shape[0], keep_o.shape[2]
            for block in range(GROUP):
                for owner in range(owners):
                    span = slice(owner * rows, (owner + 1) * rows)
                    if block < GROUP - 1:
                        value = acc[span, block * width : (block + 1) * width]
                    else:
                        value = gattn[span, :]
                    pack_block(place, block, owner, value, keep_o, send_o)


def adam_parts(weight, moment, second, gradient):
    moment = beta_one * moment + (1.0 - beta_one) * gradient
    second = beta_two * second + (1.0 - beta_two) * gradient * gradient
    first_fix = 1.0 - beta_one**STEP
    second_fix = 1.0 - beta_two**STEP
    weight = weight - (learn_rate / first_fix) * moment / (
        jnp.sqrt(second * (1.0 / second_fix)) + adam_eps
    )
    return weight, moment, second


def adam_kernel(place, *refs):
    att, mlp = refs[0:4], refs[4:8]
    weights, means, squares = refs[8:11], refs[11:14], refs[14:17]
    grads, new_w, new_m, new_s = refs[17:20], refs[20:23], refs[23:26], refs[26:29]
    width = att[0].shape[-1]

    def write(which, where, gradient):
        grads[which][where] = gradient
        result = adam_parts(
            weights[which][where], means[which][where], squares[which][where], gradient
        )
        new_w[which][where], new_m[which][where], new_s[which][where] = result

    def block_of(parts, block, offset=0):
        k = place[1] ^ block
        here, there = offset + (k >> 1), offset + 1 - (k >> 1)
        near = parts[0][here].astype(f32) + parts[1][there].astype(f32)
        far = parts[2][here].astype(f32) + parts[3][there].astype(f32)
        return jnp.where((k & 1) == 0, near, far)

    everything = slice(None)
    for block in range(GROUP):
        g_att = block_of(att, block)
        if block < GROUP - 1:
            write(0, (everything, slice(block * width, (block + 1) * width)), g_att)
        else:
            write(1, (everything, everything), g_att)
        at = (GROUP - 1 + block) * width
        write(0, (everything, slice(at, at + width)), block_of(mlp, block))
        write(2, (block,), block_of(mlp, block, 2))


def adam_mod(grad, weight, mean, square, *refs):
    grad_o, weight_o, mean_o, square_o = refs[4:]
    gradient = grad[...]
    grad_o[...] = gradient
    weight_o[...], mean_o[...], square_o[...] = adam_parts(
        weight[...], mean[...], square[...], gradient
    )


def swap(value, axis, bit):
    size = lax.axis_size(axis)
    return lax.ppermute(value, axis, [(i, i ^ bit) for i in range(size)])


def upper_stages(owners):
    half = owners // 2
    if half <= 4:
        return [list(range(1, half))]
    return [[1 << b] for b in range(half.bit_length() - 1)]


def gather_upper(held):
    for stage in upper_stages(lax.axis_size("dp")):
        held = jnp.concatenate([held] + [swap(held, "dp", 2 * c) for c in stage], axis=0)
    return held


def group_gather(value):
    two = swap(value, "group", 2)
    return value, two, swap(value, "group", 1), swap(two, "group", 1)


def in_order(parts, mine):
    low = mine < 2
    even = (mine & 1) == 0
    near, far = jnp.where(low, parts[0], parts[1]), jnp.where(low, parts[1], parts[0])
    other, wide = jnp.where(low, parts[2], parts[3]), jnp.where(low, parts[3], parts[2])
    return jnp.concatenate(
        [
            jnp.where(even, near, other),
            jnp.where(even, other, near),
            jnp.where(even, far, wide),
            jnp.where(even, wide, far),
        ],
        axis=0,
    )


def scatter_near(keep, dtype):
    half = keep.shape[0] // 2
    return keep[:half] + swap(keep[half:].astype(dtype), "dp", 1).astype(f32)


def scatter_upper(keep, dtype):
    for stage in upper_stages(lax.axis_size("dp")):
        if len(stage) == keep.shape[0] - 1:
            total = keep[0]
            for c in stage:
                total = total + swap(keep[c].astype(dtype), "dp", 2 * c).astype(f32)
            return total
        bit = stage[0]
        pairs = keep.reshape((keep.shape[0] // 2, 2) + keep.shape[1:])
        keep = pairs[:, 0] + swap(pairs[:, 1].astype(dtype), "dp", 2 * bit).astype(f32)
    return keep[0]


def share_parts(total):
    sent = total.astype(bf16)
    return [sent] + [swap(sent, "group", k) for k in (2, 1, 3)]


def to_owners(value):
    return lax.all_to_all(value, "dp", 0, 0, tiled=True)


def pad_rows(value, width, rows):
    flat = value.reshape(value.shape[0], -1)
    return jnp.pad(flat, ((0, 0), (0, rows * width - flat.shape[1]))).reshape(-1, rows, width)


def halves(value):
    high = lax.reduce_precision(value, 8, 7)
    return jnp.concatenate([high.astype(bf16), (value - high).astype(bf16)], axis=-1)


def compiler(limit=56):
    return pltpu.CompilerParams(
        dimension_semantics=("arbitrary",), vmem_limit_bytes=limit * 1024 * 1024
    )


def whole_spec(array):
    zeros = (0,) * len(array.shape)
    return pl.BlockSpec(tuple(array.shape), lambda l, *_: zeros)


def latent_spec(array):
    zeros = (0,) * (len(array.shape) - 1)
    return pl.BlockSpec((1,) + tuple(array.shape[1:]), lambda l, *_: (l,) + zeros)


def call(kernel, place, latent_args, whole_args, latent_outs, whole_outs, scratch, grid, start=0, us=15):
    def shifted(array):
        zeros = (0,) * (len(array.shape) - 1)
        return pl.BlockSpec((1,) + tuple(array.shape[1:]), lambda l, *_: (l + start,) + zeros)

    ins = [shifted(a) for a in latent_args] + [whole_spec(a) for a in whole_args]
    outs = [latent_spec(a) for a in latent_outs] + [whole_spec(a) for a in whole_outs]
    func = kernel.func if isinstance(kernel, functools.partial) else kernel
    return pl.pallas_call(
        kernel,
        grid_spec=pltpu.PrefetchScalarGridSpec(
            num_scalar_prefetch=1,
            grid=(grid,),
            in_specs=ins,
            out_specs=outs,
            scratch_shapes=scratch,
        ),
        out_shape=list(latent_outs) + list(whole_outs),
        compiler_params=compiler(),
        cost_estimate=pl.CostEstimate(
            flops=int(us * 1e9), bytes_accessed=int(us * 1e6), transcendentals=0
        ),
        name=func.__name__,
    )(place, *latent_args, *whole_args)


def like(shape, dtype):
    return jax.ShapeDtypeStruct(shape, dtype)


def body(
    latents, cotangent, timestep, labels, class_table,
    input_proj, attn_proj, mlp_down, biases,
    mean_input, mean_attn, mean_down, mean_biases,
    sq_input, sq_attn, sq_down, sq_biases,
):
    count, seq_len, width = latents.shape
    rows = input_proj.shape[0]
    owners = lax.axis_size("dp")
    hidden = mlp_down.shape[0] * owners
    heads = width // HEAD
    me = lax.axis_index("dp")
    mine = lax.axis_index("group")
    place = jnp.stack([me, mine]).astype(jnp.int32)

    core = mine & 1
    bias_shard = biases.shape[0]
    mod_at = 3 * width + hidden
    bias_mod_at = 4 * width + hidden

    def blocks_of(first, second):
        return jnp.where(core == 0, first, second)

    q_rows, k_rows, v_rows = [input_proj[:, b * width : (b + 1) * width] for b in range(3)]
    ids = jnp.concatenate([timestep, labels]).astype(jnp.int32)
    note = jnp.concatenate([biases, (ids // 32).astype(f32), (ids % 32).astype(f32)])
    note_size = note.shape[0]
    note_rows = 8 * -(-note_size // (8 * width))
    note = pad_rows(note[None].astype(bf16), width, note_rows)[0]
    message = jnp.concatenate(
        [
            blocks_of(q_rows, v_rows).astype(bf16),
            blocks_of(k_rows, attn_proj).astype(bf16),
            note,
        ],
        axis=0,
    )
    att_own = to_owners(jnp.broadcast_to(message[None], (owners,) + message.shape))
    up_rows = [input_proj[:, (3 + b) * width : (4 + b) * width] for b in range(GROUP)]
    mlp_piece = jnp.concatenate(
        [
            blocks_of(up_rows[0], up_rows[2]),
            blocks_of(up_rows[1], up_rows[3]),
            blocks_of(mlp_down[: 2 * rows], mlp_down[2 * rows :]),
        ],
        axis=0,
    ).astype(bf16)
    att_own, mlp_piece = lax.optimization_barrier((att_own, mlp_piece))
    att_other = swap(att_own, "group", 1)
    mlp_near = gather_upper(mlp_piece[None])

    notes = att_own[:, 2 * rows :].reshape(owners, -1)[:, :note_size].astype(f32)
    bias_all = notes[:, :bias_shard].reshape(1, -1)
    ids = 32.0 * notes[:, bias_shard : bias_shard + 2 * count] + notes[:, bias_shard + 2 * count :]
    times_all = ids[:, :count].reshape(-1)
    labels_all = ids[:, count:].reshape(-1).astype(jnp.int32)
    class_count = class_table.shape[0]
    one_hot = (labels_all[:, None] == jnp.arange(class_count, dtype=jnp.int32)[None, :]).astype(bf16)
    condition = time_embed(times_all, width) + dot(one_hot, class_table)
    cond_b = (condition * jax.nn.sigmoid(condition)).astype(bf16)
    w_mod = input_proj[:, mod_at:].astype(bf16)
    cond_cols = lax.dynamic_slice_in_dim(cond_b, me * rows, rows, 1)
    partial = dot(cond_cols, w_mod).reshape(owners, count, -1)
    modulation = jnp.sum(to_owners(partial), axis=0) + bias_all[:, bias_mod_at:]
    mod = modulation.reshape(count, 6, width)
    mod, mlp_near = lax.optimization_barrier((mod, mlp_near))
    mlp_far = swap(mlp_near, "dp", 1)

    qkv, attended, branch_a, lse = call(
        attn_forward, place,
        [latents, mod], [bias_all, att_own, att_other],
        [
            like((count, seq_len, 3 * width), bf16),
            like((count, seq_len, width), bf16),
            like((count, seq_len, width), f32),
            like((count, heads, seq_len), f32),
        ],
        [],
        [pltpu.VMEM((width, 4 * width), bf16), pltpu.VMEM((width, seq_len), f32)],
        count,
    )
    branch_a, mlp_near, mlp_far = lax.optimization_barrier((branch_a, mlp_near, mlp_far))
    mlp_parts = [mlp_near, mlp_far, swap(mlp_near, "group", 1), swap(mlp_far, "group", 1)]
    cond_group = [cond_cols] + [swap(cond_cols, "group", k) for k in (2, 1, 3)]
    bias_like = like((1, bias_mod_at), f32)
    block_out, d_middle, d_mod_m, g_attn, g_bias_m, mlp_keep, mlp_send = call(
        mlp_both, place,
        [latents, cotangent, branch_a, attended, mod], [bias_all] + mlp_parts,
        [
            like((count, seq_len, width), bf16),
            like((count, seq_len, width), f32),
            like((count, 6, width), f32),
        ],
        [
            like((width, width), f32),
            bias_like,
            like((owners, 4, rows, width), f32),
            like((owners, 4, rows, width), bf16),
        ],
        [
            pltpu.VMEM((width, hidden), bf16),
            pltpu.VMEM((hidden, width), bf16),
            pltpu.VMEM((seq_len, hidden), bf16),
            pltpu.VMEM((seq_len, hidden), f32),
            pltpu.VMEM((seq_len, hidden), bf16),
            pltpu.VMEM((width, hidden), f32),
            pltpu.VMEM((width, hidden), f32),
        ],
        count,
        us=20,
    )
    mlp_keep = mlp_keep + swap(mlp_send, "group", 1).astype(f32)
    d_middle, mlp_keep = lax.optimization_barrier((d_middle, mlp_keep))

    half = count // 2
    token_like = like((half, seq_len, width), f32)
    mod_like = like((half, 2, width), f32)
    gb_like = like((1, 2 * width), f32)
    scratch = [
        pltpu.VMEM((width, 4 * width), bf16),
        pltpu.VMEM((width, seq_len), f32),
        pltpu.VMEM((seq_len, 3 * width), bf16),
    ]
    token_args = [latents, d_middle, qkv, lse, mod]
    glat_0, d_mod_0, g_bias_a, acc = call(
        functools.partial(attn_backward, True, False), place,
        token_args, [att_own, att_other],
        [token_like, mod_like], [gb_like, like((width, 3 * width), f32)], scratch, half, 0, 10,
    )
    mlp_keep = scatter_near(mlp_keep, bf16)
    acc, mlp_keep = lax.optimization_barrier((acc, mlp_keep))
    glat_1, d_mod_1, g_bias_a, at_keep, at_send = call(
        functools.partial(attn_backward, False, True), place,
        token_args, [att_own, att_other, acc, g_bias_a, g_attn],
        [token_like, mod_like],
        [gb_like, like((owners, 2, rows, width), f32), like((owners, 2, rows, width), bf16)],
        scratch + [pltpu.VMEM((width, 3 * width), f32)], count - half, half, 10,
    )
    mlp_total = scatter_upper(mlp_keep, bf16)
    grad_latents = jnp.concatenate([glat_0, glat_1], axis=0)

    d_mod_a = jnp.concatenate([d_mod_0, d_mod_1], axis=0)
    d_modulation = jnp.concatenate([d_mod_a, d_mod_m[:, 2:]], axis=1).reshape(count, 6 * width)
    bias_grad = jnp.concatenate(
        [g_bias_a[0], g_bias_m[0, 2 * width :], jnp.sum(d_modulation, axis=0)]
    )
    at_keep = at_keep + swap(at_send, "group", 1).astype(f32)
    bias_grad = (bias_grad + swap(bias_grad, "group", 2)) + (
        swap(bias_grad, "group", 1) + swap(bias_grad, "group", 3)
    )

    dm_rows = count * 6
    bias_halves = halves(bias_grad.reshape(owners, bias_shard))
    tail_rows = -(-2 * bias_shard // width)
    tail_rows += -(2 * rows + dm_rows + tail_rows) % 8
    message = jnp.concatenate(
        [
            at_keep.astype(bf16).reshape(owners, 2 * rows, width),
            jnp.broadcast_to(
                d_modulation.astype(bf16).reshape(1, dm_rows, width), (owners, dm_rows, width)
            ),
            pad_rows(bias_halves, width, tail_rows),
        ],
        axis=1,
    )
    message, mlp_total = lax.optimization_barrier((message, mlp_total))
    mlp_shared = share_parts(mlp_total)
    arrived = to_owners(message)
    at_total = jnp.sum(arrived[:, : 2 * rows].astype(f32), axis=0).reshape(2, rows, width)
    at_shared = share_parts(at_total)
    dm_all = arrived[:, 2 * rows : 2 * rows + dm_rows].reshape(owners * count, 6 * width)
    dm_group = group_gather(dm_all)
    g_halves = jnp.sum(
        arrived[:, 2 * rows + dm_rows :].reshape(owners, -1)[:, : 2 * bias_shard].astype(f32), axis=0
    )
    g_biases = g_halves[:bias_shard] + g_halves[bias_shard:]
    bias_out = (g_biases,) + adam_parts(biases, mean_biases, sq_biases, g_biases)

    back = dot(dm_all, w_mod, NT).reshape(owners, count, rows)
    back = to_owners(back)
    d_cond = back.transpose(1, 0, 2).reshape(count, width)
    own_cond = lax.dynamic_slice_in_dim(condition, me * count, count, 0)
    own_sig = jax.nn.sigmoid(own_cond)
    grad_cond = d_cond * (own_sig * (1.0 + own_cond * (1.0 - own_sig)))

    steps = rows // 16 if rows % 16 == 0 else 1
    block_rows = rows // steps

    def spec_of(array):
        if len(array.shape) == 3:
            return pl.BlockSpec((array.shape[0], block_rows, width), lambda s, *_: (0, s, 0))
        return pl.BlockSpec((block_rows, min(array.shape[1], mod_at)), lambda s, *_: (s, 0))

    state = [
        entry
        for three in (
            (input_proj, attn_proj, mlp_down),
            (mean_input, mean_attn, mean_down),
            (sq_input, sq_attn, sq_down),
        )
        for entry in (three[0], three[1], three[2].reshape(GROUP, rows, width))
    ]
    args = at_shared + mlp_shared + state
    results = [like(a.shape, f32) for a in state[:3]] * 4
    outs = pl.pallas_call(
        adam_kernel,
        grid_spec=pltpu.PrefetchScalarGridSpec(
            num_scalar_prefetch=1,
            grid=(steps,),
            in_specs=[spec_of(a) for a in args],
            out_specs=[spec_of(a) for a in results],
        ),
        out_shape=results,
        compiler_params=compiler(),
        name="adam",
    )(place, *args)

    g_mod = dot(in_order(cond_group, mine), in_order(dm_group, mine), TN)
    first = mod_at // width
    local = pl.BlockSpec((rows, width), lambda s: (0, s))
    placed = pl.BlockSpec((rows, width), lambda s: (0, s + first))
    anywhere = pl.BlockSpec(memory_space=pl.ANY)
    wide = pl.pallas_call(
        adam_mod,
        grid=(6,),
        in_specs=[local] + [placed] * 3 + [anywhere] * 4,
        out_specs=[placed] * 4,
        out_shape=[like(input_proj.shape, f32)] * 4,
        input_output_aliases={4 + i: i for i in range(4)},
        compiler_params=compiler(),
        name="adam_mod",
    )(g_mod, input_proj, mean_input, sq_input, outs[0], outs[3], outs[6], outs[9])

    def flat(index):
        three = outs[3 * index : 3 * index + 3]
        return (wide[index], three[1], three[2].reshape(mlp_down.shape), bias_out[index])

    return (block_out, grad_latents, grad_cond) + flat(0) + flat(1) + flat(2) + flat(3)


def solution(mesh):
    tokens = P(("dp", "group"), None, None)
    four = (P("dp", None), P("dp", None), P("dp", None), P("dp"))
    in_specs = (tokens, tokens, P(("dp", "group")), P(("dp", "group")), P()) + four * 3
    out_specs = (tokens, tokens, P(("dp", "group"), None)) + four * 4
    return jax.shard_map(body, mesh=mesh, in_specs=in_specs, out_specs=out_specs, check_vma=False)
```

```python
import functools
import math

import jax
import jax.numpy as jnp
from jax import lax
from jax.experimental import pallas as pl
from jax.experimental.pallas import tpu as pltpu
from jax.sharding import PartitionSpec as P


HEAD = 64
STEP = 2
GROUP = 4

learn_rate = 0.01
beta_one = 0.9
beta_two = 0.999
adam_eps = 1e-08
norm_eps = 1e-06

f32 = jnp.float32
bf16 = jnp.bfloat16

NN = (((1,), (0,)), ((), ()))
NT = (((1,), (1,)), ((), ()))
TN = (((0,), (0,)), ((), ()))


def dot(left, right, dims=NN):
    return lax.dot_general(left, right, dims, preferred_element_type=f32)


def row_mean(values):
    return jnp.sum(values, axis=-1, keepdims=True) * (1.0 / values.shape[-1])


def layer_norm(values):
    centred = values - row_mean(values)
    inv_std = lax.rsqrt(row_mean(centred * centred) + norm_eps)
    return centred * inv_std, inv_std


def norm_back(gradient, normed, inv_std):
    return inv_std * (gradient - row_mean(gradient) - normed * row_mean(gradient * normed))


def token_sum(values):
    return jnp.sum(values, axis=0, keepdims=True)


def time_embed(timestep, model_width):
    half_width = model_width // 2
    frequency = jnp.exp(
        jnp.arange(half_width, dtype=f32) * (-math.log(10000.0) / half_width)
    )
    angles = timestep.astype(f32)[:, None] * frequency[None, :]
    return jnp.concatenate([jnp.cos(angles), jnp.sin(angles)], axis=1)


def spot_of(relative, owners):
    return (relative & 1) * (owners // 2) + (relative >> 1)


def each_piece(place, pieces, store):
    for block in range(GROUP):
        for k, piece in zip((0, 2, 1, 3), pieces):

            @pl.when((place[1] ^ k) == block)
            def _():
                for owner in range(piece.shape[0]):
                    store(block, owner, piece)


def unpack_attn(place, pieces, whole, base):
    width = pieces[0].shape[-1]
    rows = whole.shape[0] // pieces[0].shape[0]

    def store(block, owner, piece):
        whole[owner * rows : (owner + 1) * rows, block * width : (block + 1) * width] = piece[
            owner, base : base + rows, :
        ]

    each_piece(place, pieces, store)


def unpack_mlp(place, pieces, w_up, w_down):
    width = w_up.shape[0]
    owners = 2 * pieces[0].shape[0]
    rows = width // owners
    for core in range(2):
        for far in range(2):
            for side in range(2):
                piece = pieces[2 * far + side]

                @pl.when((place[1] & 1) == (core ^ far))
                def _():
                    for upper in range(owners // 2):
                        owner = place[0] ^ (2 * upper + side)
                        at = pl.multiple_of(owner * rows, rows)
                        for part in range(2):
                            cols = slice((2 * core + part) * width, (2 * core + part + 1) * width)
                            w_up[pl.ds(at, rows), cols] = piece[
                                upper, part * rows : (part + 1) * rows, :
                            ]
                        start = pl.multiple_of(owner * (GROUP * rows) + 2 * core * rows, rows)
                        w_down[pl.ds(start, 2 * rows), :] = piece[upper, 2 * rows : 4 * rows, :]


def unpack_mlp_rows(place, pieces, w_up, w_down):
    width = w_up.shape[0]
    owners = 2 * pieces[0].shape[0]
    rows = width // owners
    for core in range(2):
        for far in range(2):
            near_side, far_side = pieces[2 * far], pieces[2 * far + 1]

            @pl.when((place[1] & 1) == (core ^ far))
            def _():
                for owner in range(owners):
                    relative = place[0] ^ owner
                    piece = jnp.where(
                        (relative & 1) == 0, near_side[relative >> 1], far_side[relative >> 1]
                    )
                    for part in range(2):
                        block = 2 * core + part
                        w_up[
                            owner * rows : (owner + 1) * rows, block * width : (block + 1) * width
                        ] = piece[part * rows : (part + 1) * rows]
                    start = (owner * GROUP + 2 * core) * rows
                    w_down[start : start + 2 * rows, :] = piece[2 * rows : 4 * rows]


def pack_block(place, block, spot, value, keep, send, offset=0):
    k = place[1] ^ block
    half = (k >> 1) + offset

    @pl.when((k & 1) == 0)
    def _():
        keep[spot, half] = value

    @pl.when((k & 1) == 1)
    def _():
        send[spot, half] = value.astype(bf16)


def lane_masks():
    lane = lax.broadcasted_iota(jnp.int32, (1, 2 * HEAD), 1)
    low = (lane < HEAD).astype(f32)
    return low.astype(bf16), (1.0 - low).astype(bf16)


def attn_forward(base, place, lat, mod, bias, p0, p1, p2, p3, qkv_o, att_o, branch_o, lse_o, whole, att_t):
    width = lat.shape[-1]

    @pl.when(pl.program_id(0) == 0)
    def _():
        unpack_attn(place, (p0, p1, p2, p3), whole, base)

    normed, _ = layer_norm(lat[0].astype(f32))
    input_a = (normed * (1.0 + mod[0, 1:2]) + mod[0, 0:1]).astype(bf16)
    projected = dot(input_a, whole[:, : 3 * width])
    queries = (projected[:, :width] + bias[0:1, :width]).astype(bf16)
    key_vecs = projected[:, width : 2 * width].astype(bf16)
    values = (projected[:, 2 * width :] + bias[0:1, width : 2 * width]).astype(bf16)
    qkv_o[0, :, :width] = queries
    qkv_o[0, :, width : 2 * width] = key_vecs
    qkv_o[0, :, 2 * width :] = values
    values_t = values.T
    scale = 1.0 / math.sqrt(HEAD)
    masks = lane_masks()
    for pair in range(width // (2 * HEAD)):
        cols = slice(pair * 2 * HEAD, (pair + 1) * 2 * HEAD)
        for side in range(2):
            head = pair * 2 + side
            scores = dot(key_vecs[:, cols] * masks[side], queries[:, cols], NT) * scale
            peak = jnp.max(scores, axis=0, keepdims=True)
            powers = jnp.exp(scores - peak)
            total = jnp.sum(powers, axis=0, keepdims=True)
            lse_o[0, head : head + 1, :] = peak + jnp.log(total)
            probs = (powers * (1.0 / total)).astype(bf16)
            att_t[head * HEAD : (head + 1) * HEAD, :] = dot(
                values_t[head * HEAD : (head + 1) * HEAD, :], probs
            )
    attended = att_t[...].T.astype(bf16)
    att_o[0] = attended
    branch_o[0] = dot(attended, whole[:, 3 * width :]) + bias[0:1, 2 * width : 3 * width]


def mlp_both(
    base, place, lat, cot, branch, att, mod, bias,
    p0, p1, p2, p3,
    out_o, dmid_o, dmod_o, gattn_o, gbias_o, keep_o, send_o,
    w_up, w_down, gelu_s, slope_s, dpre_s, acc_up, acc_down,
):
    width = lat.shape[-1]
    hidden = w_up.shape[1]
    step = pl.program_id(0)
    first = step == 0

    @pl.when(first)
    def _():
        whole_tiles = p0.shape[1] % 64 == 0
        unpack = unpack_mlp if whole_tiles else unpack_mlp_rows
        unpack(place, (p0, p1, p2, p3), w_up, w_down)
        acc_up[...] = jnp.zeros_like(acc_up)
        acc_down[...] = jnp.zeros_like(acc_down)
        gattn_o[...] = jnp.zeros_like(gattn_o)
        gbias_o[...] = jnp.zeros_like(gbias_o)

    b_up = bias[0:1, 3 * width : 3 * width + hidden]
    b_down = bias[0:1, 3 * width + hidden : 4 * width + hidden]
    gate_a, shift_m, scale_m, gate_m = mod[0, 2:3], mod[0, 3:4], mod[0, 4:5], mod[0, 5:6]
    branch_a = branch[0]
    middle = lat[0].astype(f32) + gate_a * branch_a
    normed, inv_std = layer_norm(middle)
    input_m = (normed * (1.0 + scale_m) + shift_m).astype(bf16)
    inner = math.sqrt(2.0 / math.pi)
    chunk = 512
    for start in range(0, hidden, chunk):
        cols = slice(start, start + chunk)
        pre = dot(input_m, w_up[:, cols]) + b_up[:, cols]
        square = pre * pre
        tangent = jnp.tanh(pre * (inner + (inner * 0.044715) * square))
        upper = 0.5 * (1.0 + tangent)
        gelu_s[:, cols] = (pre * upper).astype(bf16)
        slope_s[:, cols] = upper + (0.5 * pre) * (1.0 - tangent * tangent) * (
            inner + (inner * 3.0 * 0.044715) * square
        )
    branch_m = dot(gelu_s[...], w_down[...]) + b_down
    out_o[0] = (middle + gate_m * branch_m).astype(bf16)
    grad_out = cot[0].astype(f32)
    dmod_o[0, 5:6] = token_sum(grad_out * branch_m)
    d_branch_m = grad_out * gate_m
    d_branch_mb = d_branch_m.astype(bf16)
    acc_down[...] += dot(d_branch_mb, gelu_s[...], TN)
    gbias_o[0:1, 3 * width + hidden : 4 * width + hidden] += token_sum(d_branch_m)
    for start in range(0, hidden, chunk):
        cols = slice(start, start + chunk)
        d_pre = dot(d_branch_mb, w_down[cols, :], NT) * slope_s[:, cols]
        gbias_o[0:1, 3 * width + start : 3 * width + start + chunk] += token_sum(d_pre)
        dpre_s[:, cols] = d_pre.astype(bf16)
    acc_up[...] += dot(input_m, dpre_s[...], TN)
    d_input = dot(dpre_s[...], w_up[...], NT)
    dmod_o[0, 4:5] = token_sum(d_input * normed)
    dmod_o[0, 3:4] = token_sum(d_input)
    d_middle = grad_out + norm_back(d_input * (1.0 + scale_m), normed, inv_std)
    dmid_o[0] = d_middle
    dmod_o[0, 2:3] = token_sum(d_middle * branch_a)
    d_branch_a = d_middle * gate_a
    gbias_o[0:1, 2 * width : 3 * width] += token_sum(d_branch_a)
    gattn_o[...] += dot(att[0], d_branch_a.astype(bf16), TN)

    @pl.when(step == pl.num_programs(0) - 1)
    def _():
        owners, rows = keep_o.shape[0], keep_o.shape[2]
        whole_down = acc_down[...].T
        for owner in range(owners):
            spot = spot_of(place[0] ^ owner, owners)
            for block in range(GROUP):
                value = acc_up[owner * rows : (owner + 1) * rows, block * width : (block + 1) * width]
                pack_block(place, block, spot, value, keep_o, send_o)
                start = (owner * GROUP + block) * rows
                value = whole_down[start : start + rows, :]
                pack_block(place, block, spot, value, keep_o, send_o, 2)


def attn_backward(first, last, base, place, lat, dmid, qkv, lse, mod, p0, p1, p2, p3, *refs):
    refs = list(refs)
    if not first:
        acc_i, gbias_i = refs.pop(0), refs.pop(0)
    if last:
        gattn = refs.pop(0)
    glat_o, dmod_o, gbias_o = refs.pop(0), refs.pop(0), refs.pop(0)
    if last:
        keep_o, send_o, whole, dq_t, dproj, acc = refs
    else:
        acc, whole, dq_t, dproj = refs
    width = lat.shape[-1]
    step = pl.program_id(0)

    @pl.when(step == 0)
    def _():
        unpack_attn(place, (p0, p1, p2, p3), whole, base)
        acc[...] = jnp.zeros_like(acc) if first else acc_i[...]
        gbias_o[...] = jnp.zeros_like(gbias_o) if first else gbias_i[...]

    shift_a, scale_a, gate_a = mod[0, 0:1], mod[0, 1:2], mod[0, 2:3]
    normed, inv_std = layer_norm(lat[0].astype(f32))
    input_a = (normed * (1.0 + scale_a) + shift_a).astype(bf16)
    d_middle = dmid[0]
    d_att = dot((d_middle * gate_a).astype(bf16), whole[:, 3 * width :], NT).astype(bf16)
    scale = 1.0 / math.sqrt(HEAD)
    masks = lane_masks()
    low = lax.broadcasted_iota(jnp.int32, (1, 2 * HEAD), 1) < HEAD
    keys_t = qkv[0, :, width : 2 * width].T
    for pair in range(width // (2 * HEAD)):
        cols = slice(pair * 2 * HEAD, (pair + 1) * 2 * HEAD)
        q_pair = qkv[0, :, pair * 2 * HEAD : (pair + 1) * 2 * HEAD]
        k_pair = qkv[0, :, width + pair * 2 * HEAD : width + (pair + 1) * 2 * HEAD]
        v_pair = qkv[0, :, 2 * width + pair * 2 * HEAD : 2 * width + (pair + 1) * 2 * HEAD]
        do_pair = d_att[:, cols]
        d_keys, d_values = [], []
        for side in range(2):
            head = pair * 2 + side
            scores = dot(k_pair * masks[side], q_pair, NT) * scale
            probs = jnp.exp(scores - lse[0, head : head + 1, :])
            d_values.append(dot(probs.astype(bf16), do_pair))
            d_probs = dot(v_pair * masks[side], do_pair, NT)
            delta = jnp.sum(probs * d_probs, axis=0, keepdims=True)
            d_scores = (probs * (d_probs - delta) * scale).astype(bf16)
            d_keys.append(dot(d_scores, q_pair))
            dq_t[head * HEAD : (head + 1) * HEAD, :] = dot(
                keys_t[head * HEAD : (head + 1) * HEAD, :], d_scores
            )
        d_key = jnp.where(low, d_keys[0], d_keys[1])
        d_value = jnp.where(low, d_values[0], d_values[1])
        dproj[:, width + pair * 2 * HEAD : width + (pair + 1) * 2 * HEAD] = d_key.astype(bf16)
        dproj[:, 2 * width + pair * 2 * HEAD : 2 * width + (pair + 1) * 2 * HEAD] = d_value.astype(
            bf16
        )
        gbias_o[0:1, width + pair * 2 * HEAD : width + (pair + 1) * 2 * HEAD] += token_sum(d_value)
    d_query = dq_t[...].T
    gbias_o[0:1, :width] += token_sum(d_query)
    dproj[:, :width] = d_query.astype(bf16)
    acc[...] += dot(input_a, dproj[...], TN)
    d_input = dot(dproj[...], whole[:, : 3 * width], NT)
    dmod_o[0, 1:2] = token_sum(d_input * normed)
    dmod_o[0, 0:1] = token_sum(d_input)
    glat_o[0] = d_middle + norm_back(d_input * (1.0 + scale_a), normed, inv_std)

    if last:

        @pl.when(step == pl.num_programs(0) - 1)
        def _():
            owners, rows = keep_o.shape[0], keep_o.shape[2]
            for block in range(GROUP):
                for owner in range(owners):
                    span = slice(owner * rows, (owner + 1) * rows)
                    if block < GROUP - 1:
                        value = acc[span, block * width : (block + 1) * width]
                    else:
                        value = gattn[span, :]
                    pack_block(place, block, owner, value, keep_o, send_o)


def adam_parts(weight, moment, second, gradient):
    moment = beta_one * moment + (1.0 - beta_one) * gradient
    second = beta_two * second + (1.0 - beta_two) * gradient * gradient
    first_fix = 1.0 - beta_one**STEP
    second_fix = 1.0 - beta_two**STEP
    weight = weight - (learn_rate / first_fix) * moment / (
        jnp.sqrt(second * (1.0 / second_fix)) + adam_eps
    )
    return weight, moment, second


def adam_write(refs, gradient, where):
    weight, mean, square, grad_o, weight_o, mean_o, square_o = refs
    grad_o[where] = gradient
    weight_o[where], mean_o[where], square_o[where] = adam_parts(
        weight[where], mean[where], square[where], gradient
    )


def block_of(place, parts, block, rows, offset=0):
    k = place[1] ^ block
    here, there = offset + (k >> 1), offset + 1 - (k >> 1)
    near = parts[0][here].astype(f32) + parts[1][there].astype(f32)
    far = parts[2][here].astype(f32) + parts[3][there].astype(f32)
    return jnp.where((k & 1) == 0, near, far)[:rows]


def adam_kernel(place, *refs):
    att, mlp, mods, conds = refs[0:4], refs[4:8], refs[8:12], refs[12:16]
    wide, square, down = refs[16:-1:3], refs[17:-1:3], refs[18:-1:3]
    gmod = refs[-1]
    width = att[0].shape[-1]
    rows = square[0].shape[0]
    everything = slice(None)

    @pl.when(pl.program_id(0) == 0)
    def _():
        near, across, other, far = [
            dot(cond[...], mod[...], TN) for cond, mod in zip(conds, mods)
        ]
        gmod[...] = (near + across) + (other + far)

    def columns(block):
        return (everything, slice(block * width, (block + 1) * width))

    for block in range(GROUP):
        g_att = block_of(place, att, block, rows)
        if block < GROUP - 1:
            adam_write(wide, g_att, columns(block))
        else:
            adam_write(square, g_att, (everything, everything))
        adam_write(wide, block_of(place, mlp, block, rows), columns(GROUP - 1 + block))
        adam_write(down, block_of(place, mlp, block, rows, 2), (block,))
    start = 0 if gmod.shape[0] == rows else pl.multiple_of(pl.program_id(0) * rows, rows)
    for block in range(6):
        gradient = gmod[pl.ds(start, rows), block * width : (block + 1) * width]
        adam_write(wide, gradient, columns(2 * GROUP - 1 + block))


def pack_message(keep, received, mods_m, mods_0, mods_1, bias_a, bias_m, out, dms, bias):
    owners, _, rows, width = keep.shape
    count = mods_m.shape[0]
    half = mods_0.shape[0]
    for latent in range(count):
        early = mods_0 if latent < half else mods_1
        for part in range(6):
            if part < 2:
                value = early[latent % half, part : part + 1, :]
            else:
                value = mods_m[latent, part : part + 1, :]
            dms[part * count + latent : part * count + latent + 1, :] = value
    edge = bias_a.shape[1]
    bias[0:1, :edge] = bias_a[...]
    bias[0:1, edge : bias_m.shape[1]] = bias_m[0:1, edge:]
    for part in range(6):
        at = bias_m.shape[1] + part * width
        bias[0:1, at : at + width] = token_sum(dms[part * count : (part + 1) * count, :])
    dm_rows = 6 * count
    dm_b = dms[...].astype(bf16)
    shard = bias.shape[1] // owners
    spans = [(lo, min(lo + width, shard)) for lo in range(0, shard, width)]
    tail = 2 * rows + dm_rows
    for owner in range(owners):
        for k in range(2):
            out[owner, k * rows : (k + 1) * rows, :] = (
                keep[owner, k] + received[owner, k].astype(f32)
            ).astype(bf16)
        out[owner, 2 * rows : tail, :] = dm_b
        out[owner, tail:, :] = jnp.zeros((out.shape[1] - tail, width), bf16)
        for index, (lo, hi) in enumerate(spans):
            value = bias[0:1, owner * shard + lo : owner * shard + hi]
            high = value.astype(bf16)
            low = (value - high.astype(f32)).astype(bf16)
            out[owner, tail + index : tail + index + 1, : hi - lo] = high
            at = tail + len(spans) + index
            out[owner, at : at + 1, : hi - lo] = low


def open_message(spans, arrived, share, dm_all, dms):
    owners, _, width = arrived.shape
    count = dm_all.shape[0] // owners
    dm_rows = 6 * count
    rows = (share.shape[1] - 8 * -(-spans // 8))
    share[...] = jnp.zeros(share.shape, bf16)
    for k in range(2):
        total = arrived[0, k * rows : (k + 1) * rows, :].astype(f32)
        for owner in range(1, owners):
            total = total + arrived[owner, k * rows : (k + 1) * rows, :].astype(f32)
        share[k, :rows, :] = total.astype(bf16)
    tail = 2 * rows + dm_rows
    total = jnp.zeros((spans, width), f32)
    for owner in range(owners):
        ends = arrived[owner, tail:, :].astype(f32)
        total = total + (ends[:spans] + ends[spans : 2 * spans])
    high = total.astype(bf16)
    share[0, rows : rows + spans, :] = high
    share[1, rows : rows + spans, :] = (total - high.astype(f32)).astype(bf16)
    for owner in range(owners):
        block = arrived[owner, 2 * rows : tail, :].astype(f32)
        for part in range(6):
            dms[owner * count : (owner + 1) * count, part * width : (part + 1) * width] = block[
                part * count : (part + 1) * count
            ]
    dm_all[...] = dms[...].astype(bf16)


def swap(value, axis, bit):
    size = lax.axis_size(axis)
    return lax.ppermute(value, axis, [(i, i ^ bit) for i in range(size)])


def upper_stages(owners):
    half = owners // 2
    if half <= 4:
        return [list(range(1, half))]
    return [[1 << b] for b in range(half.bit_length() - 1)]


def gather_upper(held):
    for stage in upper_stages(lax.axis_size("dp")):
        held = jnp.concatenate([held] + [swap(held, "dp", 2 * c) for c in stage], axis=0)
    return held


def scatter_near(keep, dtype):
    half = keep.shape[0] // 2
    return keep[:half] + swap(keep[half:].astype(dtype), "dp", 1).astype(f32)


def scatter_upper(keep, dtype):
    for stage in upper_stages(lax.axis_size("dp")):
        if len(stage) == keep.shape[0] - 1:
            total = keep[0]
            for c in stage:
                total = total + swap(keep[c].astype(dtype), "dp", 2 * c).astype(f32)
            return total
        bit = stage[0]
        pairs = keep.reshape((keep.shape[0] // 2, 2) + keep.shape[1:])
        keep = pairs[:, 0] + swap(pairs[:, 1].astype(dtype), "dp", 2 * bit).astype(f32)
    return keep[0]


def share_parts(total):
    sent = total.astype(bf16)
    return [sent] + [swap(sent, "group", k) for k in (2, 1, 3)]


def to_owners(value):
    return lax.all_to_all(value, "dp", 0, 0, tiled=True)


def pad_rows(value, width, rows):
    flat = value.reshape(value.shape[0], -1)
    return jnp.pad(flat, ((0, 0), (0, rows * width - flat.shape[1]))).reshape(-1, rows, width)


def compiler(limit=56):
    return pltpu.CompilerParams(
        dimension_semantics=("arbitrary",), vmem_limit_bytes=limit * 1024 * 1024
    )


def whole_spec(array):
    zeros = (0,) * len(array.shape)
    return pl.BlockSpec(tuple(array.shape), lambda l, *_: zeros)


def latent_spec(array):
    zeros = (0,) * (len(array.shape) - 1)
    return pl.BlockSpec((1,) + tuple(array.shape[1:]), lambda l, *_: (l,) + zeros)


def piece_spec(array, start, size):
    owners, _, width = array.shape
    if size % 16 == 0 and start % size == 0:
        return pl.BlockSpec((owners, size, width), lambda l, *_: (0, start // size, 0)), 0
    return whole_spec(array), start


def call(kernel, place, latent_args, whole_args, pieces, extra_args, latent_outs, whole_outs, scratch,
         grid, part, start=0, us=15, options=()):
    def shifted(array):
        zeros = (0,) * (len(array.shape) - 1)
        return pl.BlockSpec((1,) + tuple(array.shape[1:]), lambda l, *_: (l + start,) + zeros)

    spec, base = piece_spec(pieces[0], *part) if part else (whole_spec(pieces[0]), 0)
    ins = [shifted(a) for a in latent_args] + [whole_spec(a) for a in whole_args]
    ins = ins + [spec] * len(pieces) + [whole_spec(a) for a in extra_args]
    outs = [latent_spec(a) for a in latent_outs] + [whole_spec(a) for a in whole_outs]
    return pl.pallas_call(
        functools.partial(kernel, *options, base),
        grid_spec=pltpu.PrefetchScalarGridSpec(
            num_scalar_prefetch=1,
            grid=(grid,),
            in_specs=ins,
            out_specs=outs,
            scratch_shapes=scratch,
        ),
        out_shape=list(latent_outs) + list(whole_outs),
        compiler_params=compiler(),
        cost_estimate=pl.CostEstimate(
            flops=int(us * 1e9), bytes_accessed=int(us * 1e6), transcendentals=0
        ),
    )(place, *latent_args, *whole_args, *pieces, *extra_args)


def like(shape, dtype):
    return jax.ShapeDtypeStruct(shape, dtype)


def body(
    latents, cotangent, timestep, labels, class_table,
    input_proj, attn_proj, mlp_down, biases,
    mean_input, mean_attn, mean_down, mean_biases,
    sq_input, sq_attn, sq_down, sq_biases,
):
    count, seq_len, width = latents.shape
    rows = input_proj.shape[0]
    owners = lax.axis_size("dp")
    hidden = mlp_down.shape[0] * owners
    heads = width // HEAD
    me = lax.axis_index("dp")
    mine = lax.axis_index("group")
    place = jnp.stack([me, mine]).astype(jnp.int32)

    bias_shard = biases.shape[0]
    mod_at = 3 * width + hidden
    bias_mod_at = 4 * width + hidden

    def block_here(blocks):
        return jnp.where(
            mine < 2,
            jnp.where(mine == 0, blocks[0], blocks[1]),
            jnp.where(mine == 2, blocks[2], blocks[3]),
        ).astype(bf16)

    columns = [input_proj[:, b * width : (b + 1) * width] for b in range(3 + GROUP)]
    ids = jnp.concatenate([timestep, labels]).astype(jnp.int32)
    note = jnp.concatenate([biases, (ids // 32).astype(f32), (ids % 32).astype(f32)])
    note_size = note.shape[0]
    note_rows = 8 * -(-note_size // (8 * width))
    message = jnp.concatenate(
        [
            block_here(columns[:3] + [attn_proj]),
            pad_rows(note[None].astype(bf16), width, note_rows)[0],
        ],
        axis=0,
    )
    att_part = (0, rows)
    pieces = to_owners(jnp.broadcast_to(message[None], (owners,) + message.shape))
    pieces_y = swap(pieces, "group", 2)

    even = (mine & 1) == 0
    mlp_piece = jnp.concatenate(
        [
            jnp.where(even, columns[3], columns[5]),
            jnp.where(even, columns[4], columns[6]),
            jnp.where(even, mlp_down[: 2 * rows], mlp_down[2 * rows :]),
        ],
        axis=0,
    ).astype(bf16)
    mlp_near = gather_upper(mlp_piece[None])
    mlp_far = swap(mlp_near, "dp", 1)

    notes = pieces[:, rows :].reshape(owners, -1)[:, :note_size].astype(f32)
    bias_all = notes[:, :bias_shard].reshape(1, -1)
    ids = 32.0 * notes[:, bias_shard : bias_shard + 2 * count] + notes[:, bias_shard + 2 * count :]
    times_all = ids[:, :count].reshape(-1)
    labels_all = ids[:, count:].reshape(-1).astype(jnp.int32)
    class_count = class_table.shape[0]
    one_hot = (labels_all[:, None] == jnp.arange(class_count, dtype=jnp.int32)[None, :]).astype(bf16)
    condition = time_embed(times_all, width) + dot(one_hot, class_table)
    cond_b = (condition * jax.nn.sigmoid(condition)).astype(bf16)
    w_mod = input_proj[:, mod_at:].astype(bf16)
    cond_cols = lax.dynamic_slice_in_dim(cond_b, me * rows, rows, 1)
    partial = dot(cond_cols, w_mod).reshape(owners, count, -1)
    partial = to_owners(partial)
    mod = (jnp.sum(partial, axis=0) + bias_all[:, bias_mod_at:]).reshape(count, 6, width)
    pieces = [pieces, pieces_y, swap(pieces, "group", 1), swap(pieces_y, "group", 1)]

    qkv, attended, branch_a, lse = call(
        attn_forward, place,
        [latents, mod], [bias_all], pieces, [],
        [
            like((count, seq_len, 3 * width), bf16),
            like((count, seq_len, width), bf16),
            like((count, seq_len, width), f32),
            like((count, heads, seq_len), f32),
        ],
        [],
        [pltpu.VMEM((width, 4 * width), bf16), pltpu.VMEM((width, seq_len), f32)],
        count, att_part,
    )
    cond_group = [cond_cols] + [swap(cond_cols, "group", k) for k in (2, 1, 3)]
    mlp_parts = [mlp_near, mlp_far, swap(mlp_near, "group", 1), swap(mlp_far, "group", 1)]
    bias_like = like((1, bias_mod_at), f32)
    block_out, d_middle, d_mod_m, g_attn, g_bias_m, mlp_keep, mlp_send = call(
        mlp_both, place,
        [latents, cotangent, branch_a, attended, mod], [bias_all], mlp_parts, [],
        [
            like((count, seq_len, width), bf16),
            like((count, seq_len, width), f32),
            like((count, 6, width), f32),
        ],
        [
            like((width, width), f32),
            bias_like,
            like((owners, 4, rows, width), f32),
            like((owners, 4, rows, width), bf16),
        ],
        [
            pltpu.VMEM((width, hidden), bf16),
            pltpu.VMEM((hidden, width), bf16),
            pltpu.VMEM((seq_len, hidden), bf16),
            pltpu.VMEM((seq_len, hidden), f32),
            pltpu.VMEM((seq_len, hidden), bf16),
            pltpu.VMEM((width, hidden), f32),
            pltpu.VMEM((width, hidden), f32),
        ],
        count, None,
        us=20,
    )
    mlp_keep = mlp_keep + swap(mlp_send, "group", 1).astype(f32)
    d_middle, mlp_keep, g_bias_m = lax.optimization_barrier((d_middle, mlp_keep, g_bias_m))

    half = count // 2
    token_like = like((half, seq_len, width), f32)
    mod_like = like((half, 2, width), f32)
    gb_like = like((1, 2 * width), f32)
    scratch = [
        pltpu.VMEM((width, 4 * width), bf16),
        pltpu.VMEM((width, seq_len), f32),
        pltpu.VMEM((seq_len, 3 * width), bf16),
    ]
    token_args = [latents, d_middle, qkv, lse, mod]
    glat_0, d_mod_0, g_bias_a, acc = call(
        attn_backward, place,
        token_args, [], pieces, [],
        [token_like, mod_like], [gb_like, like((width, 3 * width), f32)],
        scratch, half, att_part, 0, 10, (True, False),
    )
    mlp_keep = scatter_near(mlp_keep, bf16)
    acc, mlp_keep = lax.optimization_barrier((acc, mlp_keep))
    glat_1, d_mod_1, g_bias_a, at_keep, at_send = call(
        attn_backward, place,
        token_args, [], pieces, [acc, g_bias_a, g_attn],
        [token_like, mod_like],
        [gb_like, like((owners, 2, rows, width), f32), like((owners, 2, rows, width), bf16)],
        scratch + [pltpu.VMEM((width, 3 * width), f32)],
        count - half, att_part, half, 10, (False, True),
    )
    mlp_total = scatter_upper(mlp_keep, bf16)
    grad_latents = jnp.concatenate([glat_0, glat_1], axis=0)

    dm_rows = count * 6
    spans = -(-bias_shard // width)
    tail_rows = 2 * spans
    tail_rows += -(2 * rows + dm_rows + tail_rows) % 8
    at_received = swap(at_send, "group", 1)
    message = pl.pallas_call(
        pack_message,
        out_shape=like((owners, 2 * rows + dm_rows + tail_rows, width), bf16),
        scratch_shapes=[pltpu.VMEM((dm_rows, width), f32), pltpu.VMEM((1, bias_shard * owners), f32)],
        compiler_params=pltpu.CompilerParams(vmem_limit_bytes=56 * 1024 * 1024),
        name="pack_message",
    )(at_keep, at_received, d_mod_m, d_mod_0, d_mod_1, g_bias_a, g_bias_m)
    arrived = to_owners(message)
    mlp_shared = share_parts(mlp_total)
    at_total, dm_all = pl.pallas_call(
        functools.partial(open_message, spans),
        out_shape=[
            like((2, rows + 8 * -(-spans // 8), width), bf16),
            like((owners * count, 6 * width), bf16),
        ],
        scratch_shapes=[pltpu.VMEM((owners * count, 6 * width), f32)],
        compiler_params=pltpu.CompilerParams(vmem_limit_bytes=56 * 1024 * 1024),
        name="open_message",
    )(arrived)
    at_shared = share_parts(at_total)
    dm_group = [dm_all] + [swap(dm_all, "group", k) for k in (2, 1, 3)]
    near, across, other, wide = [
        jnp.sum(part[:, rows : rows + spans].astype(f32).reshape(2, -1)[:, :bias_shard], axis=0)
        for part in at_shared
    ]
    g_biases = (near + across) + (other + wide)
    bias_out = (g_biases,) + adam_parts(biases, mean_biases, sq_biases, g_biases)

    back = dot(dm_all, w_mod, NT).reshape(owners, count, rows)
    back = to_owners(back)
    d_cond = back.transpose(1, 0, 2).reshape(count, width)
    own_cond = lax.dynamic_slice_in_dim(condition, me * count, count, 0)
    own_sig = jax.nn.sigmoid(own_cond)
    grad_cond = d_cond * (own_sig * (1.0 + own_cond * (1.0 - own_sig)))

    steps = rows // 16 if rows % 16 == 0 else 1

    def spec_of(array):
        if len(array.shape) == 3:
            size = rows // steps
            if steps == 1:
                size = array.shape[1]
            return pl.BlockSpec((array.shape[0], size, width), lambda s, *_: (0, s, 0))
        return pl.BlockSpec((rows // steps, array.shape[1]), lambda s, *_: (s, 0))

    state = []
    for three in (
        (input_proj, attn_proj, mlp_down),
        (mean_input, mean_attn, mean_down),
        (sq_input, sq_attn, sq_down),
    ):
        state += [three[0], three[1], three[2].reshape(GROUP, rows, width)]
    args = at_shared + mlp_shared + dm_group + cond_group + state
    in_specs = [spec_of(a) for a in at_shared + mlp_shared]
    in_specs += [whole_spec(a) for a in dm_group + cond_group] + [spec_of(a) for a in state]
    results = [like(a.shape, f32) for a in state[:3]] * 4
    outs = pl.pallas_call(
        adam_kernel,
        grid_spec=pltpu.PrefetchScalarGridSpec(
            num_scalar_prefetch=1,
            grid=(steps,),
            in_specs=in_specs,
            out_specs=[spec_of(a) for a in results],
            scratch_shapes=[pltpu.VMEM((rows, 6 * width), f32)],
        ),
        out_shape=results,
        compiler_params=compiler(),
        name="adam",
    )(place, *args)
    wide, square, down = outs[0::3], outs[1::3], outs[2::3]

    def flat(index):
        return (wide[index], square[index], down[index].reshape(mlp_down.shape), bias_out[index])

    return (block_out, grad_latents, grad_cond) + flat(0) + flat(1) + flat(2) + flat(3)


def solution(mesh):
    tokens = P(("dp", "group"), None, None)
    four = (P("dp", None), P("dp", None), P("dp", None), P("dp"))
    in_specs = (tokens, tokens, P(("dp", "group")), P(("dp", "group")), P()) + four * 3
    out_specs = (tokens, tokens, P(("dp", "group"), None)) + four * 4

    return jax.shard_map(body, mesh=mesh, in_specs=in_specs, out_specs=out_specs, check_vma=False)
```
